32 devices in a mesh: groups: 1, section: 32 (over z, y, x, core).
Axes of the slice: x: 2, y: 2, z: 4, core: 2. Of those that a mesh axis runs over, the one named last changes fastest.
Arguments:
- queries: bfloat16 [256, 4096], P(('groups', 'section')), may hold values from -170 to 170, as said below
- key_value_cache: bfloat16 [2, 32768, 512], P(None, ('groups', 'section')), may hold values from -6 to 6, as said below
- block_ids: int32 [256, 8], P(('groups', 'section')), may hold values from 0 to 511, as said below
- block_len: int32 [512], P(('groups', 'section')), may hold values from 1 to 64
- residual_in: bfloat16 [256, 2048], P(('groups', 'section')), may hold values from -6 to 6
- out_weight: bfloat16 [4096, 2048], P('section'), may hold values from -0.375 to 0.375
- norm_gain: float32 [2048], replicated, may hold values from 0.1 to 1.9
- expert_ids: int32 [256, 8], P(('groups', 'section')), may hold values from 0 to 31, all different within a row; in each aligned block of 8 rows (0 to 7, 8 to 15, ...) at most 2 rows name the same one
- route_weight: float32 [256, 8], P(('groups', 'section')), may hold values from 0.05 to 0.5
- w_gate: bfloat16 [32, 2048, 768], P('section'), may hold values from -0.125 to 0.125
- w_up: bfloat16 [32, 2048, 768], P('section'), may hold values from -0.125 to 0.125
- w_down: bfloat16 [32, 768, 2048], P('section'), may hold values from -0.21875 to 0.21875
Outputs:
- attn_proj: bfloat16 [256, 2048], P(('groups', 'section'))
- layer_out: bfloat16 [256, 2048], P(('groups', 'section'))
The draws below stay inside these ranges and needn't reach their ends.
Inputs may be any that keep to these rules, and one draw needn't show every extreme that they name: queries lie within the printed range. key_value_cache lies within the printed range. `block_ids`: block b belongs to device b // 16. Row r's j-th block lies in the j-th of 8 equal ranges of the pool. A device's rows fall into runs of 4 rows in order (the last run may be shorter); no two blocks read by the rows of one run lie on the same device. `expert_ids`: each row names 8 different experts; among the rows of one device no expert is named more than 2 times.
All inputs are finite; a program needn't handle non-finite values.
Results may differ from the reference program's by a relative error of at most 0.008.
Values may be sent and summed in bfloat16 or wider, within the bound.
No kernel may reach another device: no remote copies, remote signals or barrier semaphores. Data moves between devices by JAX's collectives and lax.ppermute only.
A program may use at most 128 MiB of HBM per device.

```python
import math
import jax
import jax.numpy as jnp
import numpy as np
from jax import lax

D = 2048
QUERY_HEADS = 32
KEY_VALUE_HEADS = 4
HEAD_WIDTH = 128
FFE = 768
TOPK = 8
CAP = 2
BLOCK_TOKENS = 64
PICKED_BLOCKS = 8
BLK_DEV = 16
ROW_DEV = 8
EXPERTS = 32
DECODE_ROWS = 256
POOL_BLOCKS = 512
CACHE_TOKENS = 32768
N_SECTION = 32


def blocks_helper(key):
    eighth = N_SECTION // PICKED_BLOCKS
    runs = (ROW_DEV + eighth - 1) // eighth
    base_key = jax.random.fold_in(key, 11)
    subkeys = jax.random.split(base_key, N_SECTION * PICKED_BLOCKS * runs)

    def draw_one(single_key):
        return jax.random.permutation(single_key, eighth)
    chosen = jax.vmap(draw_one)(subkeys).reshape(N_SECTION, PICKED_BLOCKS, runs * eighth)[:, :, :ROW_DEV]
    within = jax.random.randint(jax.random.fold_in(key, 12), (N_SECTION, PICKED_BLOCKS, ROW_DEV), 0, BLK_DEV)
    part_index = jnp.arange(PICKED_BLOCKS).reshape(1, PICKED_BLOCKS, 1)
    device = part_index * eighth + chosen
    block_position = device * BLK_DEV + within
    return jnp.transpose(block_position, (0, 2, 1)).reshape(DECODE_ROWS, PICKED_BLOCKS).astype(jnp.int32)


def cache_helper(key):
    random_noise_key = jax.random.fold_in(key, 22)
    cache_pool = jnp.clip(jax.random.normal(random_noise_key, (2, CACHE_TOKENS, KEY_VALUE_HEADS * HEAD_WIDTH), jnp.float32), -5.0, 5.0)
    return cache_pool


def draw_block_ids(key, part):
    return blocks_helper(key)


def draw_key_value_cache(key, part):
    return cache_helper(key).astype(jnp.bfloat16)


def draw_queries(key, part):
    drawn = jnp.clip(jax.random.normal(jax.random.fold_in(key, 33), (DECODE_ROWS, QUERY_HEADS * HEAD_WIDTH), jnp.float32), -5.0, 5.0)
    return drawn.astype(jnp.bfloat16)


def touch_ends(values, rng, smallest, high):
    spot = [jax.random.randint(jax.random.fold_in(rng, axis), (), 0, length) for axis, length in enumerate(values.shape)]
    longest = values.shape.index(max(values.shape))
    neighbour = spot[:longest] + [(spot[longest] + 1) % values.shape[longest]] + spot[longest + 1:]
    return values.at[tuple(spot)].set(smallest).at[tuple(neighbour)].set(high)


def block_levels(key, shape, shards, smallest, top_value):
    gain = 1.0
    for axis_at, parts in shards:
        draws = jax.random.uniform(jax.random.fold_in(jax.random.fold_in(key, 6), axis_at), (parts,), jnp.float32, smallest / len(shards), top_value / len(shards))
        gain = gain * jnp.repeat(jnp.exp(draws), shape[axis_at] // parts).reshape((-1,) + (1,) * (len(shape) - 1 - axis_at))
    return gain


def assign_block(key, own, number, rows, amount, top, most, slope):
    order = jax.random.permutation(key, amount)
    crowded, ordinary = portions_of(amount, rows * top, most, slope, True), portions_of(amount, rows * top, most, slope, False)
    places = jnp.arange(amount)

    def named(tallies, turn):
        used = int((tallies > 0).sum())
        fixed = max(1, used // 4)
        moved = fixed + (places - fixed + turn * (used - fixed)) % max(1, amount - fixed)
        return jnp.zeros((amount,), jnp.int32).at[order[jnp.where(places < fixed, places, moved)]].set(jnp.asarray(tallies, jnp.int32))

    tallies = jnp.where(number % 4 == 0, named(crowded, number // 4), named(ordinary, number - number // 4 - 1))
    mixed = jax.random.permutation(jax.random.fold_in(own, 3), amount)
    giver, sink = mixed[0:amount // 2 * 2:2], mixed[1:amount // 2 * 2:2]
    slack = jnp.minimum(tallies[giver] - 1, most - tallies[sink]) // 2
    slack = jnp.where((giver == order[0]) | (sink == order[0]) | (tallies[sink] == 0), 0, jnp.maximum(slack, 0))
    moved = jax.random.randint(jax.random.fold_in(own, 4), (amount // 2,), 0, 1 << 20) % (slack + 1)
    tallies = tallies.at[giver].add(-moved).at[sink].add(moved)
    items = jnp.searchsorted(jnp.cumsum(tallies), jnp.arange(rows * top), side="right").astype(jnp.int32)
    grid = items.reshape(top, rows).T
    grid = grid[jax.random.permutation(jax.random.fold_in(own, 1), rows)]
    turn = jax.random.randint(jax.random.fold_in(own, 2), (rows, 1), 0, top)
    return jnp.take_along_axis(grid, (jnp.arange(top)[None, :] + turn) % top, axis=1)


def portions_of(number_of, total, bound, lean, full):
    weights = [(1 << 20) // math.isqrt(rank ** lean) + 1 for rank in range(1, number_of + 1)]
    largest = bound if full else min(bound, max(-(-total // number_of), total * weights[0] // sum(weights)))
    least = 1 if total - largest >= number_of - 1 else 0
    given, spare = [largest] + [least] * (number_of - 1), total - largest - least * (number_of - 1)
    while spare > 0:
        candidates = [i for i in range(1, number_of) if given[i] < largest] or [i for i in range(1, number_of) if given[i] < bound]
        whole, left = sum([weights[i] for i in candidates]), spare
        for i in candidates:
            extra = min(bound - given[i], max(1, left * weights[i] // whole), spare)
            given[i] = given[i] + extra
            spare = spare - extra
    return np.array(given)


def centred(rng, dims, deviation, reach, cuts=(), held_as=jnp.bfloat16):
    factor_of = block_levels(rng, dims, cuts, -0.22, 0.18) if cuts else 1.0
    values = jax.random.normal(rng, dims, jnp.float32) * deviation * factor_of
    return jnp.minimum(jnp.maximum(values, -reach), reach).astype(held_as)


def setup_inputs(seed: int = 0, part: int = 0) -> dict:
    key_of = jax.random.split(jax.random.key(seed), 13)
    own_keys = jax.random.split(jax.random.fold_in(key_of[12], part), 13)
    queries = draw_queries(jax.random.fold_in(jax.random.fold_in(key_of[12], part), 71), part)
    key_value_cache = draw_key_value_cache(jax.random.fold_in(jax.random.fold_in(key_of[12], part), 71), part)
    block_ids = draw_block_ids(jax.random.fold_in(jax.random.fold_in(key_of[12], part), 71), part)
    block_len = touch_ends(jax.random.randint(own_keys[3], (POOL_BLOCKS,), 1, BLOCK_TOKENS + 1), jax.random.fold_in(own_keys[3], 1), 1, BLOCK_TOKENS).astype(jnp.int32)
    residual_in = centred(own_keys[4], (DECODE_ROWS, D), 1.0, 6.0, ((0, 32),))
    out_weight = centred(key_of[5], (QUERY_HEADS * HEAD_WIDTH, D), (4.0 * (QUERY_HEADS * HEAD_WIDTH) ** -0.5), 0.375, ((0, 32),))
    norm_gain = jnp.clip(1.0 + 0.18 * jax.random.normal(key_of[6], (D,), jnp.float32), 0.1, 1.9)
    expert_ids_keys = jax.random.split(jax.random.fold_in(own_keys[7], 1), DECODE_ROWS // ROW_DEV)
    expert_ids_turns = jax.random.permutation(jax.random.fold_in(own_keys[7], 3), DECODE_ROWS // ROW_DEV)
    expert_ids = jax.vmap(lambda own, number: assign_block(jax.random.fold_in(own_keys[7], 2), own, number, ROW_DEV, EXPERTS, TOPK, CAP, 2))(expert_ids_keys, expert_ids_turns).reshape((DECODE_ROWS, TOPK))
    route_weight = jnp.clip(jnp.exp(math.log(0.5) - 2.3025851 * jax.random.uniform(own_keys[8], (DECODE_ROWS, TOPK), jnp.float32) ** block_levels(own_keys[8], (DECODE_ROWS, TOPK), ((0, 32),), -0.2, 0.2)), 0.05, 0.5)
    w_gate = centred(key_of[9], (EXPERTS, D, FFE), D ** -0.5, 0.125, ((0, 32),))
    w_up = centred(key_of[10], (EXPERTS, D, FFE), D ** -0.5, 0.125, ((0, 32),))
    w_down = centred(key_of[11], (EXPERTS, FFE, D), FFE ** -0.5, 0.21875, ((0, 32),))
    return dict(queries=queries, key_value_cache=key_value_cache, block_ids=block_ids, block_len=block_len, residual_in=residual_in, out_weight=out_weight, norm_gain=norm_gain, expert_ids=expert_ids, route_weight=route_weight, w_gate=w_gate, w_up=w_up, w_down=w_down)


def attend_row(single_query_row, index_row, key_value_cache, block_len):
    group_width = QUERY_HEADS // KEY_VALUE_HEADS
    query_head_rows = single_query_row.astype(jnp.float32).reshape(KEY_VALUE_HEADS, group_width, HEAD_WIDTH)

    def take_block(first_token):
        return lax.dynamic_slice_in_dim(key_value_cache, first_token, BLOCK_TOKENS, 1)
    block_list = jax.vmap(take_block)((index_row * BLOCK_TOKENS).astype(jnp.int32))
    key_matrix = block_list[:, 0].astype(jnp.float32).reshape(PICKED_BLOCKS, BLOCK_TOKENS, KEY_VALUE_HEADS, HEAD_WIDTH)
    value_matrix = block_list[:, 1].astype(jnp.float32).reshape(PICKED_BLOCKS, BLOCK_TOKENS, KEY_VALUE_HEADS, HEAD_WIDTH)
    scores = jnp.einsum('kgd,btkd->bkgt', query_head_rows, key_matrix, precision=lax.Precision.HIGHEST) * HEAD_WIDTH ** (-0.5)
    lengths = block_len[index_row]
    is_valid = jnp.arange(BLOCK_TOKENS)[None, :] < lengths[:, None]
    token_mask = is_valid[:, None, None, :]
    block_peak = lax.optimization_barrier(jnp.max(jnp.where(token_mask, scores, -1e+30), axis=-1))
    weights = jnp.where(token_mask, jnp.exp(scores - block_peak[..., None]), 0.0).astype(jnp.bfloat16)
    weights = lax.optimization_barrier(weights).astype(jnp.float32)
    totals = lax.optimization_barrier(jnp.sum(weights, axis=-1))
    weighted = jnp.einsum('bkgt,btkd->bkgd', weights, value_matrix, precision=lax.Precision.HIGHEST)
    overall = lax.optimization_barrier(jnp.max(block_peak, axis=0))
    factor = jnp.exp(block_peak - overall[None])
    numerator = lax.optimization_barrier(jnp.sum(factor[..., None] * weighted, axis=0))
    denominator = lax.optimization_barrier(jnp.sum(factor * totals, axis=0))
    return (numerator / denominator[..., None]).reshape(QUERY_HEADS * HEAD_WIDTH).astype(jnp.bfloat16)

def reference(queries, key_value_cache, block_ids, block_len, residual_in, out_weight, norm_gain, expert_ids, route_weight, w_gate, w_up, w_down):
    attention = lax.map(lambda packed: attend_row(packed[0], packed[1], key_value_cache, block_len), (queries, block_ids))
    projected = jnp.dot(attention, out_weight, preferred_element_type=jnp.float32).astype(jnp.bfloat16)
    stream = residual_in.astype(jnp.float32) + projected.astype(jnp.float32)
    normed = (stream * lax.rsqrt(lax.optimization_barrier(jnp.mean(stream * stream, axis=-1, keepdims=True)) + 1e-06) * norm_gain).astype(jnp.bfloat16)
    assign = ROW_DEV * TOPK
    chosen = expert_ids.reshape(N_SECTION, assign)
    same_expert = chosen[:, :, None] == chosen[:, None, :]
    earlier = jnp.arange(assign)[:, None] > jnp.arange(assign)[None, :]
    slot_index = lax.optimization_barrier(jnp.sum(same_expert & earlier[None], axis=2)).astype(jnp.int32)
    position = (jnp.arange(N_SECTION, dtype=jnp.int32)[:, None] * CAP + slot_index).reshape(-1).astype(jnp.int32)
    flat_expert = expert_ids.reshape(-1)
    row_of = (jnp.arange(DECODE_ROWS * TOPK) // TOPK).astype(jnp.int32)
    gathered_rows = normed[row_of]
    flat_weight = route_weight.reshape(-1)
    slots_all = N_SECTION * CAP

    def one_expert(moe_acc, packed):
        expert_id, gate_mat, up_mat, down_mat = packed
        is_mine = flat_expert == expert_id
        target = jnp.where(is_mine, position, slots_all).astype(jnp.int32)
        buffer = jnp.zeros((slots_all, D), jnp.bfloat16).at[target].set(gathered_rows, mode='drop')
        gate_act = jnp.dot(buffer, gate_mat, preferred_element_type=jnp.float32)
        up_act = jnp.dot(buffer, up_mat, preferred_element_type=jnp.float32)
        hidden = (jax.nn.silu(gate_act) * up_act).astype(jnp.bfloat16)
        result = jnp.dot(hidden, down_mat, preferred_element_type=jnp.float32).astype(jnp.bfloat16)
        picked_blocks = result[jnp.minimum(position, slots_all - 1)].astype(jnp.float32)
        scaled = jnp.where(is_mine, flat_weight, 0.0)[:, None] * picked_blocks
        return (moe_acc + lax.optimization_barrier(jnp.sum(scaled.reshape(DECODE_ROWS, TOPK, D), axis=1)), None)
    moe_sum = lax.scan(one_expert, jnp.zeros((DECODE_ROWS, D), jnp.float32), (jnp.arange(EXPERTS, dtype=jnp.int32), w_gate, w_up, w_down))[0]
    layer_out = (stream + moe_sum).astype(jnp.bfloat16)
    return (projected, layer_out)
```

```python
import functools

import jax
import jax.numpy as jnp
from jax import lax
from jax.experimental import pallas as pl
from jax.experimental.pallas import tpu as pltpu
from jax.sharding import PartitionSpec as P

HEADS = 32
KV_HEADS = 4
WIDTH = 128
CAP = 2
BLOCK_TOKENS = 64
LANES = 128
GROUP = 2
STATS = 8
NEG = -1e30
BF = jnp.bfloat16
F32 = jnp.float32

VM = pl.BlockSpec(memory_space=pltpu.VMEM)
SM = pl.BlockSpec(memory_space=pltpu.SMEM)


def call(kernel, out_shape, in_specs, scratch, name, flops=0, nbytes=0, outs=None):
    return pl.pallas_call(
        kernel,
        out_shape=out_shape,
        in_specs=in_specs,
        out_specs=outs if outs is not None else jax.tree.map(lambda _: VM, out_shape),
        scratch_shapes=scratch,
        name=name,
        cost_estimate=pl.CostEstimate(flops=flops, bytes_accessed=nbytes, transcendentals=0),
    )


def pack_kernel(run, slots, blocks, ids, q, out, qs, meta):
    rows = q.shape[0]
    picks = ids.shape[1]
    for h in range(HEADS):
        qs[pl.ds(h, rows, stride=HEADS), :] = q[:, h * WIDTH:(h + 1) * WIDTH].astype(F32)
    meta[...] = jnp.zeros_like(meta)
    if rows * picks != out.shape[0] * slots:
        out[...] = jnp.zeros_like(out)
    lane = lax.broadcasted_iota(jnp.int32, (1, LANES), 1)
    for r in range(rows):
        tile = qs[r * HEADS:(r + 1) * HEADS, :].astype(BF)
        slot = r // run
        for j in range(picks):
            b = ids[r, j]
            dev = lax.div(b, blocks)
            local = b - dev * blocks
            out[dev, slot * HEADS:(slot + 1) * HEADS, :] = tile
            meta[dev, slot:slot + 1, :] = jnp.where(
                lane == 0, local + 1, jnp.where(lane == 1, r % run, 0)
            ).astype(F32)
    out[:, slots * HEADS:, :] = meta[...].astype(BF)


def attend_kernel(n, slots, g, hg, lens, x, kv, out, qf, qb, mf, bias, sc, wb, st):
    blocks = lens.shape[0]
    tokens = kv.shape[1]
    pairs = n * slots
    per = pairs // g
    cnt = n // g
    ngrp = n // g
    qrows = slots * HEADS
    gw = HEADS // KV_HEADS

    def unpack(d, _):
        base = pl.multiple_of(d * qrows, qrows)
        qf[pl.ds(base, qrows), :] = x[d, 0:qrows, :].astype(F32)
        mb = pl.multiple_of(d * 8, 8)
        mf[pl.ds(mb, 8), :] = x[d, qrows:qrows + 8, :].astype(F32)
        return 0

    lax.fori_loop(0, n, unpack, 0, unroll=4)

    def heads(h, _):
        parts = []
        for i in range(g):
            for q in range(slots):
                parts.append(qf[pl.ds(i * qrows + q * HEADS + h, cnt, stride=g * qrows), :])
        base = pl.multiple_of(h * pairs, pairs)
        qb[pl.ds(base, pairs), :] = jnp.concatenate(parts, axis=0).astype(BF)
        return 0

    lax.fori_loop(0, HEADS, heads, 0, unroll=4)

    parts = []
    for i in range(g):
        for q in range(slots):
            parts.append(mf[pl.ds(i * 8 + q, cnt, stride=g * 8), :])
    mp = jnp.concatenate(parts, axis=0)
    blk = mp[:, 0:1].astype(jnp.int32) - 1
    rr = mp[:, 1:2]
    length = jnp.zeros_like(blk)
    for b in range(blocks):
        length = jnp.where(blk == b, lens[b], length)
    first = blk * BLOCK_TOKENS
    last = first + length
    tok = lax.broadcasted_iota(jnp.int32, (pairs, tokens), 1)
    bias[...] = jnp.where((tok >= first) & (tok < last), 0.0, NEG)
    st[...] = jnp.zeros_like(st)
    lane = lax.broadcasted_iota(jnp.int32, (pairs, HEADS * STATS), 1)

    def kv_head(k, _):
        off = pl.multiple_of(k * WIDTH, WIDTH)
        qbase = pl.multiple_of(k * (gw * pairs), gw * pairs)
        sc[...] = lax.dot_general(
            qb[pl.ds(qbase, gw * pairs), :], kv[0, :, pl.ds(off, WIDTH)],
            (((1,), (1,)), ((), ())), preferred_element_type=F32)

        def soft(hh, _):
            base = pl.multiple_of(hh * pairs, pairs)
            s = sc[pl.ds(base, pairs), :] * (WIDTH ** -0.5) + bias[...]
            m = jnp.max(s, axis=-1, keepdims=True)
            m = jnp.maximum(m, -1e20).astype(BF).astype(F32)
            w = jnp.exp(s - m).astype(BF)
            wb[pl.ds(base, pairs), :] = w
            l = jnp.sum(w.astype(F32), axis=-1, keepdims=True)
            hi = l.astype(BF).astype(F32)
            h = k * gw + hh
            at = lax.rem(h, hg) * (ngrp * STATS) + lax.div(h, hg) * STATS
            st[...] = jnp.where(lane == at, m, jnp.where(
                lane == at + 1, hi, jnp.where(
                    lane == at + 2, l - hi, jnp.where(lane == at + 3, rr, st[...]))))
            return 0

        lax.fori_loop(0, gw, soft, 0)
        o = jnp.dot(wb[...], kv[1, :, pl.ds(off, WIDTH)], preferred_element_type=F32)
        for hh in range(gw):
            h = k * gw + hh
            grp = lax.div(h, hg)
            if gw % hg == 0:
                inner = hh % hg
                for i in range(g):
                    r0 = hh * pairs + i * per
                    out[grp * g + i, inner * per:(inner + 1) * per, :] = o[r0:r0 + per, :].astype(BF)
            else:
                raise ValueError("group heads")
        return 0

    lax.fori_loop(0, KV_HEADS, kv_head, 0)

    tt = jnp.concatenate(
        [jnp.transpose(st[:, a:a + LANES]) for a in range(0, HEADS * STATS, LANES)], axis=0)
    span = ngrp * STATS
    copies = LANES // (hg * per)
    for i in range(g):
        row = jnp.concatenate(
            [tt[hh * span:(hh + 1) * span, i * per:(i + 1) * per] for hh in range(hg)] * copies, axis=1)
        for grp in range(ngrp):
            out[grp * g + i, hg * per:, :] = row[grp * STATS:(grp + 1) * STATS, :].astype(BF)


def project_kernel(n, slots, g, hg, run, rows, x, wo, wo2, out, sf, cm, ws):
    pairs = n * slots
    per = pairs // g
    span = hg * per
    cnt = n // g
    fw = wo.shape[0]
    par = lax.rem(lax.axis_index("section"), 2)
    ws[pl.ds(pl.multiple_of(par * fw, fw), fw), :] = wo[...]
    ws[pl.ds(pl.multiple_of((1 - par) * fw, fw), fw), :] = wo2[...]
    sf[...] = x[:, span:, :].astype(F32).reshape(n * STATS, LANES)
    m = sf[pl.ds(0, n, stride=STATS), :]
    l = sf[pl.ds(1, n, stride=STATS), :] + sf[pl.ds(2, n, stride=STATS), :]
    rid = sf[pl.ds(3, n, stride=STATS), :]
    peak = jnp.zeros_like(m)
    for r in range(run):
        mine = rid == r
        top = jnp.max(jnp.where(mine, m, -3e38), axis=0, keepdims=True)
        peak = jnp.where(mine, top, peak)
    f = jnp.exp(m - peak)
    fl = f * l
    den = jnp.ones_like(m)
    for r in range(run):
        mine = rid == r
        tot = jnp.sum(jnp.where(mine, fl, 0.0), axis=0, keepdims=True)
        den = jnp.where(mine, tot, den)
    c = f / den
    lane = lax.broadcasted_iota(jnp.int32, (n, LANES), 1)
    inner = lax.rem(lane, span)
    hh = lax.div(inner, per)
    pl_ = lax.rem(inner, per)
    q = lax.div(pl_, cnt)
    s = lax.rem(pl_, cnt)
    local = rows * cnt
    target = hh * local + s * rows + q * run + rid.astype(jnp.int32)
    dpt = LANES // span
    total = hg * local
    row = lax.broadcasted_iota(jnp.int32, (total, LANES), 0)
    side = lax.div(lax.broadcasted_iota(jnp.int32, (1, LANES), 1), span)
    for t in range(n // dpt):
        blk_c = c[t * dpt:t * dpt + 1, :]
        blk_t = target[t * dpt:t * dpt + 1, :]
        for u in range(1, dpt):
            d = t * dpt + u
            blk_c = jnp.where(side == u, c[d:d + 1, :], blk_c)
            blk_t = jnp.where(side == u, target[d:d + 1, :], blk_t)
        cm[:, t * LANES:(t + 1) * LANES] = jnp.where(row == blk_t, blk_c, 0.0).astype(BF)
    a = x[:, 0:span, :].reshape(n * span, LANES)
    att = jnp.dot(cm[...], a, preferred_element_type=F32).astype(BF)
    att = jnp.concatenate([att[i * local:(i + 1) * local, :] for i in range(hg)], axis=1)
    for col in range(0, ws.shape[1], 512):
        p = jnp.dot(att, ws[:, col:col + 512], preferred_element_type=F32)
        out[:, :, col:col + 512] = p.reshape(cnt, rows, 512).astype(BF)


def norm_kernel(eid, slot, x, res, gain, proj, out, nf):
    rows, width = res.shape
    acc = x[0].astype(F32)
    for i in range(1, x.shape[0]):
        acc = acc + x[i].astype(F32)
    p = acc.astype(BF)
    proj[...] = p
    stream = res[...].astype(F32) + p.astype(F32)
    ms = jnp.mean(stream * stream, axis=-1, keepdims=True)
    nrm = stream * lax.rsqrt(ms + 1e-06) * gain[...]
    tiles = width // LANES
    for c in range(tiles):
        nf[pl.ds(c, rows, stride=tiles), :] = nrm[:, c * LANES:(c + 1) * LANES]
    if rows * eid.shape[1] != out.shape[0] * CAP:
        out[...] = jnp.zeros_like(out)
    for r in range(rows):
        tile = nf[r * tiles:(r + 1) * tiles, :].astype(BF)
        for k in range(eid.shape[1]):
            out[eid[r, k], slot[r, k]] = tile


def expert_kernel(x, wg, wu, wd, out, xf, xb, of, gb, ub, db, sg, su, sd):
    n, cap, tiles, _ = x.shape
    m = n * cap
    width, ffe = wg.shape[0], wg.shape[1]
    kc = width // 4
    fc = ffe // 3
    gate = [pltpu.make_async_copy(wg.at[pl.ds(i * kc, kc)], gb.at[pl.ds(i * kc, kc)], sg.at[i]) for i in range(4)]
    up = [pltpu.make_async_copy(wu.at[pl.ds(i * kc, kc)], ub.at[pl.ds(i * kc, kc)], su.at[i]) for i in range(4)]
    down = [pltpu.make_async_copy(wd.at[pl.ds(i * fc, fc)], db.at[pl.ds(i * fc, fc)], sd.at[i]) for i in range(3)]
    for a, b in zip(gate, up):
        a.start()
        b.start()
    for a in down:
        a.start()
    xf[...] = x[...].astype(F32).reshape(m * tiles, LANES)
    for c in range(tiles):
        xb[:, c * LANES:(c + 1) * LANES] = xf[pl.ds(c, m, stride=tiles), :].astype(BF)
    ga = jnp.zeros((m, ffe), F32)
    ua = jnp.zeros((m, ffe), F32)
    for i in range(4):
        xs = xb[:, i * kc:(i + 1) * kc]
        gate[i].wait()
        ga = ga + jnp.dot(xs, gb[i * kc:(i + 1) * kc, :], preferred_element_type=F32)
        up[i].wait()
        ua = ua + jnp.dot(xs, ub[i * kc:(i + 1) * kc, :], preferred_element_type=F32)
    h = (ga / (1.0 + jnp.exp(-ga)) * ua).astype(BF)
    for a in down:
        a.wait()
    for c in range(0, width, 512):
        o = jnp.dot(h, db[:, c:c + 512], preferred_element_type=F32)
        for t in range(4):
            of[pl.ds(c // LANES + t, m, stride=tiles), :] = o[:, t * LANES:(t + 1) * LANES]
    out[...] = of[...].astype(BF).reshape(n, cap, tiles, LANES)


def finish_kernel(eid, slot, rw, x, res, proj, out, acc):
    rows, width = res.shape
    tiles = width // LANES
    for r in range(rows):
        a = jnp.zeros((tiles, LANES), F32)
        for k in range(eid.shape[1]):
            a = a + rw[r, k] * x[eid[r, k], slot[r, k]].astype(F32)
        acc[r * tiles:(r + 1) * tiles, :] = a
    for c in range(tiles):
        sl = slice(c * LANES, (c + 1) * LANES)
        stream = res[:, sl].astype(F32) + proj[:, sl].astype(F32)
        out[:, sl] = (stream + acc[pl.ds(c, rows, stride=tiles), :]).astype(BF)


def shards(
    queries,
    key_value_cache,
    block_ids,
    block_len,
    residual_in,
    out_weight,
    norm_gain,
    expert_ids,
    route_weight,
    w_gate,
    w_up,
    w_down,
):
    n = lax.axis_size("section")
    rows, qwidth = queries.shape
    picks = block_ids.shape[1]
    blocks = block_len.shape[0]
    width = residual_in.shape[1]
    tokens = key_value_cache.shape[1]
    run = n // picks
    slots = (rows + run - 1) // run
    g = GROUP
    fw = out_weight.shape[0]
    hg = g * fw // WIDTH
    pairs = n * slots
    per = pairs // g
    span = hg * per
    cnt = n // g
    tiles = width // LANES
    gw = HEADS // KV_HEADS
    a2a = functools.partial(
        lax.all_to_all, axis_name="section", split_axis=0, concat_axis=0, tiled=True)
    sds = jax.ShapeDtypeStruct

    other_weight = lax.ppermute(out_weight, "section", [(i, i ^ 1) for i in range(n)])
    flat = expert_ids.reshape(-1)
    order = jnp.arange(flat.shape[0])
    slot = jnp.sum(
        (flat[:, None] == flat[None, :]) & (order[:, None] > order[None, :]), axis=1
    ).astype(jnp.int32).reshape(expert_ids.shape)

    chunk = slots * HEADS + 8
    sent = call(
        functools.partial(pack_kernel, run, slots, blocks),
        sds((n, chunk, LANES), BF), [SM, VM],
        [pltpu.VMEM((rows * HEADS, LANES), F32), pltpu.VMEM((n, 8, LANES), F32)],
        "pack", nbytes=n * chunk * LANES * 2,
    )(block_ids, queries)
    asked = a2a(sent)
    parts = call(
        functools.partial(attend_kernel, n, slots, g, hg),
        sds((n, span + STATS, LANES), BF), [SM, VM, VM],
        [
            pltpu.VMEM((pairs * HEADS, LANES), F32),
            pltpu.VMEM((pairs * HEADS, LANES), BF),
            pltpu.VMEM((n * 8, LANES), F32),
            pltpu.VMEM((pairs, tokens), F32),
            pltpu.VMEM((gw * pairs, tokens), F32),
            pltpu.VMEM((gw * pairs, tokens), BF),
            pltpu.VMEM((pairs, HEADS * STATS), F32),
        ],
        "attend", flops=4 * HEADS * pairs * tokens * WIDTH, nbytes=1 << 22,
    )(block_len, asked, key_value_cache)
    back = a2a(parts)
    local = rows * cnt
    partial = call(
        functools.partial(project_kernel, n, slots, g, hg, run, rows),
        sds((cnt, rows, width), BF), [VM, VM, VM],
        [
            pltpu.VMEM((n * STATS, LANES), F32),
            pltpu.VMEM((hg * local, n * span), BF),
            pltpu.VMEM((g * fw, width), BF),
        ],
        "project", flops=2 * local * g * fw * width, nbytes=1 << 21,
    )(back, out_weight, other_weight)
    summed = a2a(partial, axis_index_groups=[[s * g + i for s in range(cnt)] for i in range(g)])
    experts = n * w_gate.shape[0]
    attn_proj, routed = call(
        norm_kernel,
        (sds((rows, width), BF), sds((experts, CAP, tiles, LANES), BF)), [SM, SM, VM, VM, VM],
        [pltpu.VMEM((rows * tiles, LANES), F32)],
        "norm", nbytes=1 << 20,
    )(expert_ids, slot, summed, residual_in, norm_gain.reshape(1, width))
    arrived = a2a(routed)
    ffe = w_gate.shape[2]
    hbm = pl.BlockSpec(memory_space=pl.ANY)
    slots_in = n * CAP

    def run_expert(xin, wg, wu, wd):
        return call(
            expert_kernel,
            sds((n, CAP, tiles, LANES), BF), [VM, hbm, hbm, hbm],
            [
                pltpu.VMEM((slots_in * tiles, LANES), F32),
                pltpu.VMEM((slots_in, width), BF),
                pltpu.VMEM((slots_in * tiles, LANES), F32),
                pltpu.VMEM((width, ffe), BF),
                pltpu.VMEM((width, ffe), BF),
                pltpu.VMEM((ffe, width), BF),
                pltpu.SemaphoreType.DMA((4,)),
                pltpu.SemaphoreType.DMA((4,)),
                pltpu.SemaphoreType.DMA((3,)),
            ],
            "experts", flops=6 * slots_in * width * ffe, nbytes=6 * width * ffe,
        )(xin, wg, wu, wd)

    per_device = w_gate.shape[0]
    if per_device == 1:
        done = run_expert(arrived, w_gate[0], w_up[0], w_down[0])
    else:
        split = arrived.reshape(n, per_device, CAP, tiles, LANES)
        done = jnp.stack(
            [run_expert(split[:, e], w_gate[e], w_up[e], w_down[e]) for e in range(per_device)], axis=1
        ).reshape(arrived.shape)
    returned = a2a(done)
    layer_out = call(
        finish_kernel,
        sds((rows, width), BF), [SM, SM, SM, VM, VM, VM],
        [pltpu.VMEM((rows * tiles, LANES), F32)],
        "finish", nbytes=1 << 19,
    )(expert_ids, slot, route_weight, returned, residual_in, attn_proj)
    return (attn_proj, layer_out)


def solution(mesh):
    both = P(("groups", "section"), None)
    placed = (
        both,
        P(None, ("groups", "section"), None),
        both,
        P(("groups", "section")),
        both,
        P("section", None),
        P(),
        both,
        both,
        P("section", None, None),
        P("section", None, None),
        P("section", None, None),
    )
    return jax.shard_map(
        shards,
        mesh=mesh,
        in_specs=placed,
        out_specs=(both, both),
        check_vma=False,
    )
```

```python
import functools

import jax
import jax.numpy as jnp
from jax import lax
from jax.experimental import pallas as pl
from jax.experimental.pallas import tpu as pltpu
from jax.sharding import PartitionSpec as P


HEADS = 32
KV_HEADS = 4
WIDTH = 128
CAP = 2
BLOCK_TOKENS = 64
LANES = 128
GROUP = 4
STATS = 8
BATCH = 16
NEG = -1e30
COST = 1 << 26
GATE_PARTS = 3
DOWN_PARTS = 4
BF = jnp.bfloat16
F32 = jnp.float32

VM = pl.BlockSpec(memory_space=pltpu.VMEM)
SM = pl.BlockSpec(memory_space=pltpu.SMEM)
HB = pl.BlockSpec(memory_space=pltpu.HBM)
ANY = pl.BlockSpec(memory_space=pl.ANY)


def call(kernel, out_shape, in_specs, scratch, flops=0, nbytes=0, room=8):
    return pl.pallas_call(
        kernel,
        out_shape=out_shape,
        in_specs=in_specs,
        out_specs=jax.tree.map(lambda _: VM, out_shape),
        scratch_shapes=scratch,
        compiler_params=pltpu.CompilerParams(vmem_limit_bytes=room << 20),
        cost_estimate=pl.CostEstimate(flops=flops, bytes_accessed=nbytes, transcendentals=0),
    )


def stage_kernel(count, *refs):
    sem = refs[-1]
    outs = refs[-1 - count:-1]
    copies = [pltpu.make_async_copy(refs[i], outs[i], sem.at[i]) for i in range(count)]
    for c in copies:
        c.start()
    for c in copies:
        c.wait()


def stage(*arrays, after=()):
    count = len(arrays)
    nbytes = sum(a.size * a.dtype.itemsize for a in arrays)
    return call(
        functools.partial(stage_kernel, count),
        tuple(jax.ShapeDtypeStruct(a.shape, a.dtype) for a in arrays),
        [ANY] * (count + len(after)), [pltpu.SemaphoreType.DMA((count,))],
        nbytes=nbytes,
    )(*arrays, *after)


def gather_kernel(*refs):
    sem = refs[-1]
    out = refs[-2]
    parts = refs[:-2]
    fw = parts[0].shape[0]
    me = lax.rem(lax.axis_index("section"), len(parts))
    copies = []
    for i, part in enumerate(parts):
        at = pl.multiple_of(lax.bitwise_xor(me, i) * fw, fw)
        copies.append(pltpu.make_async_copy(part, out.at[pl.ds(at, fw)], sem.at[i]))
    for c in copies:
        c.start()
    for c in copies:
        c.wait()


def pack_kernel(run, slots, blocks, ids_in, q_in, out, ids, q, qs, meta, sem):
    rows = q.shape[0]
    picks = ids.shape[1]
    get_ids = pltpu.make_async_copy(ids_in, ids, sem.at[0])
    get_q = pltpu.make_async_copy(q_in, q, sem.at[1])
    get_ids.start()
    get_q.start()
    get_q.wait()
    for h in range(HEADS):
        qs[pl.ds(h, rows, stride=HEADS), :] = q[:, h * WIDTH:(h + 1) * WIDTH].astype(F32)
    meta[...] = jnp.zeros_like(meta)
    get_ids.wait()
    if rows * picks != out.shape[0] * slots:
        out[...] = jnp.zeros_like(out)
    lane = lax.broadcasted_iota(jnp.int32, (1, LANES), 1)
    for r in range(rows):
        tile = qs[r * HEADS:(r + 1) * HEADS, :].astype(BF)
        slot = r // run
        for j in range(picks):
            b = ids[r, j]
            dev = lax.div(b, blocks)
            local = b - dev * blocks
            out[dev, slot * HEADS:(slot + 1) * HEADS, :] = tile
            meta[dev, slot:slot + 1, :] = jnp.where(
                lane == 0, local + 1, jnp.where(lane == 1, r % run, 0)
            ).astype(F32)
    out[:, slots * HEADS:, :] = meta[...].astype(BF)


def attend_kernel(n, slots, g, hg, lens_in, x, kv, out, lens, mv, ms, of, mx, sg, sem):
    get_lens = pltpu.make_async_copy(lens_in, lens, sem.at[1])
    get_lens.start()
    pairs = n * slots
    per = pairs // g
    cnt = n // g
    ngrp = n // g
    qrows = slots * HEADS
    gw = HEADS // KV_HEADS
    span = hg * per

    mv[...] = x[:, qrows:qrows + 8, :].astype(F32).reshape(n * 8, LANES).astype(jnp.int32)
    table = pltpu.make_async_copy(mv, ms, sem.at[0])
    table.start()
    sg[...] = jnp.zeros_like(sg)
    table.wait()
    get_lens.wait()
    lane = lax.broadcasted_iota(jnp.int32, (HEADS, LANES), 1)
    column = lax.broadcasted_iota(jnp.int32, (HEADS, KV_HEADS * BLOCK_TOKENS), 1)
    owner = lax.div(lax.broadcasted_iota(jnp.int32, column.shape, 0), gw)
    tok = jnp.where(lax.div(column, BLOCK_TOKENS) == owner, lax.rem(column, BLOCK_TOKENS), BLOCK_TOKENS)

    def some(step, carry):
        todo = []
        for d in range(BATCH):
            dev = step * BATCH + d
            for q in range(slots):
                blk = ms[dev * 8 + q, 0] - 1
                safe = jnp.maximum(blk, 0)
                length = jnp.where(blk >= 0, lens[safe], 0)
                base = pl.multiple_of(safe * BLOCK_TOKENS, BLOCK_TOKENS)
                pos = lax.rem(dev, g) * per + q * cnt + lax.div(dev, g)
                todo.append((dev, q, length, base, pos, ms[dev * 8 + q, 1]))
        scores = []
        for dev, q, length, base, pos, rr in todo:
            kb = kv[0, pl.ds(base, BLOCK_TOKENS), :]
            kc = jnp.concatenate([kb[:, k * WIDTH:(k + 1) * WIDTH] for k in range(KV_HEADS)], axis=0)
            scores.append(lax.dot_general(
                x[dev, q * HEADS:(q + 1) * HEADS, :], kc,
                (((1,), (1,)), ((), ())), preferred_element_type=F32))
        soft = []
        for s, (dev, q, length, base, pos, rr) in zip(scores, todo):
            s = jnp.where(tok < length, s * (WIDTH ** -0.5), NEG)
            m = jnp.max(s, axis=-1, keepdims=True)
            w = jnp.where(tok < length, jnp.exp(s - m), 0.0).astype(BF)
            l = jnp.sum(w.astype(F32), axis=-1, keepdims=True)
            soft.append((m, w, l))
        for (m, w, l), (dev, q, length, base, pos, rr) in zip(soft, todo):
            vb = kv[1, pl.ds(base, BLOCK_TOKENS), :]
            vc = jnp.concatenate([vb[:, k * WIDTH:(k + 1) * WIDTH] for k in range(KV_HEADS)], axis=0)
            of[pl.ds(pl.multiple_of(pos * HEADS, HEADS), HEADS), :] = jnp.dot(
                w, vc, preferred_element_type=F32)
        top, tot, who = carry
        for (m, w, l), (dev, q, length, base, pos, rr) in zip(soft, todo):
            here = lane == pos
            top = jnp.where(here, m, top)
            tot = jnp.where(here, l, tot)
            who = jnp.where(here, rr.astype(F32), who)
        return top, tot, who

    zero = jnp.zeros((HEADS, LANES), F32)
    top, tot, who = lax.fori_loop(0, n // BATCH, some, (zero, zero, zero))

    def heads(h, _):
        grp = lax.div(h, hg)
        at = pl.multiple_of(lax.rem(h, hg) * per, per)
        for i in range(g):
            rows = of[pl.ds(i * per * HEADS + h, per, stride=HEADS), :].astype(BF)
            out[grp * g + i, pl.ds(at, per), :] = rows
        return 0

    lax.fori_loop(0, HEADS, heads, 0, unroll=4)

    hi = top.astype(BF).astype(F32)
    mid = (top - hi).astype(BF).astype(F32)
    big = tot.astype(BF).astype(F32)
    copies = LANES // span
    for t, v in enumerate((hi, mid, top - hi - mid, big, tot - big, who)):
        mx[...] = v
        for i in range(g):
            row = jnp.concatenate(
                [mx[pl.ds(hh, ngrp, stride=hg), :][:, i * per:(i + 1) * per] for hh in range(hg)] * copies, axis=1)
            sg[pl.ds(i * STATS + t, ngrp, stride=g * STATS), :] = row
    out[:, span:, :] = sg[...].reshape(n, STATS, LANES).astype(BF)


def attend(n, slots, g, hg, block_len, asked, key_value_cache):
    pairs = n * slots
    span = hg * (pairs // g)
    sds = jax.ShapeDtypeStruct
    return call(
        functools.partial(attend_kernel, n, slots, g, hg),
        sds((n, span + STATS, LANES), BF), [HB, VM, VM],
        [
            pltpu.SMEM(block_len.shape, jnp.int32),
            pltpu.VMEM((n * 8, LANES), jnp.int32),
            pltpu.SMEM((n * 8, LANES), jnp.int32),
            pltpu.VMEM((pairs * HEADS, LANES), F32),
            pltpu.VMEM((HEADS, LANES), F32),
            pltpu.VMEM((n * STATS, LANES), F32),
            pltpu.SemaphoreType.DMA((2,)),
        ],
        flops=4 * HEADS * pairs * BLOCK_TOKENS * WIDTH, nbytes=COST,
    )(block_len, asked, key_value_cache)


def project_kernel(n, slots, g, hg, run, rows, x, ws, out, sf, cm):
    pairs = n * slots
    per = pairs // g
    span = hg * per
    cnt = n // g
    sf[...] = x[:, span:, :].astype(F32).reshape(n * STATS, LANES)
    m = (sf[pl.ds(0, n, stride=STATS), :] + sf[pl.ds(1, n, stride=STATS), :]
         + sf[pl.ds(2, n, stride=STATS), :])
    l = sf[pl.ds(3, n, stride=STATS), :] + sf[pl.ds(4, n, stride=STATS), :]
    rid = sf[pl.ds(5, n, stride=STATS), :]
    peak = jnp.zeros_like(m)
    for r in range(run):
        mine = rid == r
        top = jnp.max(jnp.where(mine, m, -3e38), axis=0, keepdims=True)
        peak = jnp.where(mine, top, peak)
    f = jnp.exp(m - peak)
    fl = f * l
    den = jnp.ones_like(m)
    for r in range(run):
        mine = rid == r
        tot = jnp.sum(jnp.where(mine, fl, 0.0), axis=0, keepdims=True)
        den = jnp.where(mine, tot, den)
    c = f / den
    lane = lax.broadcasted_iota(jnp.int32, (n, LANES), 1)
    inner = lax.rem(lane, span)
    hh = lax.div(inner, per)
    pl_ = lax.rem(inner, per)
    q = lax.div(pl_, cnt)
    s = lax.rem(pl_, cnt)
    local = rows * cnt
    target = hh * local + s * rows + q * run + rid.astype(jnp.int32)
    dpt = LANES // span
    total = hg * local
    row = lax.broadcasted_iota(jnp.int32, (total, LANES), 0)
    side = lax.div(lax.broadcasted_iota(jnp.int32, (1, LANES), 1), span)
    for t in range(n // dpt):
        blk_c = c[t * dpt:t * dpt + 1, :]
        blk_t = target[t * dpt:t * dpt + 1, :]
        for u in range(1, dpt):
            d = t * dpt + u
            blk_c = jnp.where(side == u, c[d:d + 1, :], blk_c)
            blk_t = jnp.where(side == u, target[d:d + 1, :], blk_t)
        cm[:, t * LANES:(t + 1) * LANES] = jnp.where(row == blk_t, blk_c, 0.0).astype(BF)
    a = x[:, 0:span, :].reshape(n * span, LANES)
    att = jnp.dot(cm[...], a, preferred_element_type=F32).astype(BF)
    att = jnp.concatenate([att[i * local:(i + 1) * local, :] for i in range(hg)], axis=1)
    for col in range(0, ws.shape[1], 512):
        p = jnp.dot(att, ws[:, col:col + 512], preferred_element_type=F32)
        out[:, :, col:col + 512] = p.reshape(cnt, rows, 512).astype(BF)


def norm_kernel(eid, slot, x, res, gain, proj, out, nf):
    rows, width = res.shape
    acc = x[0].astype(F32)
    for i in range(1, x.shape[0]):
        acc = acc + x[i].astype(F32)
    p = acc.astype(BF)
    proj[...] = p
    stream = res[...].astype(F32) + p.astype(F32)
    ms = jnp.mean(stream * stream, axis=-1, keepdims=True)
    nrm = stream * lax.rsqrt(ms + 1e-06) * gain[...]
    tiles = width // LANES
    for c in range(tiles):
        nf[pl.ds(c, rows, stride=tiles), :] = nrm[:, c * LANES:(c + 1) * LANES]
    if rows * eid.shape[1] != out.shape[0] * CAP:
        out[...] = jnp.zeros_like(out)
    for r in range(rows):
        tile = nf[r * tiles:(r + 1) * tiles, :].astype(BF)
        for k in range(eid.shape[1]):
            out[eid[r, k], slot[r, k]] = tile


def expert_kernel(x, wu, wg, wd, out, xf, xb, of, gb, db, sg, sd):
    n, cap, tiles, _ = x.shape
    m = n * cap
    width, ffe = wu.shape
    gc = ffe // GATE_PARTS
    dc = width // DOWN_PARTS
    gate = [pltpu.make_async_copy(
        wg.at[:, pl.ds(i * gc, gc)], gb.at[:, pl.ds(i * gc, gc)], sg.at[i]) for i in range(GATE_PARTS)]
    down = [pltpu.make_async_copy(
        wd.at[:, pl.ds(i * dc, dc)], db.at[:, pl.ds(i * dc, dc)], sd.at[i]) for i in range(DOWN_PARTS)]
    for c in gate + down:
        c.start()
    xf[...] = x[...].astype(F32).reshape(m * tiles, LANES)
    for c in range(tiles):
        xb[:, c * LANES:(c + 1) * LANES] = xf[pl.ds(c, m, stride=tiles), :].astype(BF)
    ua = jnp.dot(xb[...], wu[...], preferred_element_type=F32)
    parts = []
    for i, c in enumerate(gate):
        c.wait()
        ga = jnp.dot(xb[...], gb[:, i * gc:(i + 1) * gc], preferred_element_type=F32)
        parts.append((ga / (1.0 + jnp.exp(-ga)) * ua[:, i * gc:(i + 1) * gc]).astype(BF))
    h = jnp.concatenate(parts, axis=1)
    for i, c in enumerate(down):
        c.wait()
        o = jnp.dot(h, db[:, i * dc:(i + 1) * dc], preferred_element_type=F32)
        for t in range(dc // LANES):
            of[pl.ds(i * dc // LANES + t, m, stride=tiles), :] = o[:, t * LANES:(t + 1) * LANES]
    out[...] = of[...].astype(BF).reshape(n, cap, tiles, LANES)


def finish_kernel(eid, slot, rw, x, res, proj, out, acc):
    rows, width = res.shape
    tiles = width // LANES
    for r in range(rows):
        a = jnp.zeros((tiles, LANES), F32)
        for k in range(eid.shape[1]):
            a = a + rw[r, k] * x[eid[r, k], slot[r, k]].astype(F32)
        acc[r * tiles:(r + 1) * tiles, :] = a
    for c in range(tiles):
        sl = slice(c * LANES, (c + 1) * LANES)
        stream = res[:, sl].astype(F32) + proj[:, sl].astype(F32)
        out[:, sl] = (stream + acc[pl.ds(c, rows, stride=tiles), :]).astype(BF)


def shards(
    queries,
    key_value_cache,
    block_ids,
    block_len,
    residual_in,
    out_weight,
    norm_gain,
    expert_ids,
    route_weight,
    w_gate,
    w_up,
    w_down,
):
    n = lax.axis_size("section")
    rows, _ = queries.shape
    picks = block_ids.shape[1]
    blocks = block_len.shape[0]
    width = residual_in.shape[1]
    run = n // picks
    slots = (rows + run - 1) // run
    g = GROUP
    fw = out_weight.shape[0]
    hg = g * fw // WIDTH
    pairs = n * slots
    per = pairs // g
    span = hg * per
    cnt = n // g
    tiles = width // LANES
    a2a = functools.partial(
        lax.all_to_all, axis_name="section", split_axis=0, concat_axis=0, tiled=True)
    sds = jax.ShapeDtypeStruct

    pieces = [out_weight]
    step = g // 2
    while step:
        pieces = pieces + [
            lax.ppermute(p, "section", [(i, i ^ step) for i in range(n)]) for p in pieces]
        step //= 2
    order = [0]
    step = g // 2
    while step:
        order = order + [o ^ step for o in order]
        step //= 2
    pieces = [pieces[order.index(i)] for i in range(g)]
    wide_weight = call(
        gather_kernel, sds((g * fw, width), BF), [ANY] * g,
        [pltpu.SemaphoreType.DMA((g,))], nbytes=g * fw * width * 4,
    )(*pieces)
    (cache,) = stage(key_value_cache)
    flat = expert_ids.reshape(-1)
    place = jnp.arange(flat.shape[0])
    slot = jnp.sum(
        (flat[:, None] == flat[None, :]) & (place[:, None] > place[None, :]), axis=1
    ).astype(jnp.int32).reshape(expert_ids.shape)

    chunk = slots * HEADS + 8
    sent = call(
        functools.partial(pack_kernel, run, slots, blocks),
        sds((n, chunk, LANES), BF), [HB, HB],
        [
            pltpu.SMEM(block_ids.shape, jnp.int32),
            pltpu.VMEM(queries.shape, BF),
            pltpu.VMEM((rows * HEADS, LANES), F32),
            pltpu.VMEM((n, 8, LANES), F32),
            pltpu.SemaphoreType.DMA((2,)),
        ],
        nbytes=COST, room=60,
    )(block_ids, queries)
    asked = a2a(sent)
    parts = attend(n, slots, g, hg, block_len, asked, cache)
    back = a2a(parts)
    local = rows * cnt
    partial = call(
        functools.partial(project_kernel, n, slots, g, hg, run, rows),
        sds((cnt, rows, width), BF), [VM, VM],
        [
            pltpu.VMEM((n * STATS, LANES), F32),
            pltpu.VMEM((hg * local, n * span), BF),
        ],
        flops=2 * local * g * fw * width, nbytes=COST,
    )(back, wide_weight)
    summed = a2a(partial, axis_index_groups=[[s * g + i for s in range(cnt)] for i in range(g)])
    experts = n * w_gate.shape[0]
    attn_proj, routed = call(
        norm_kernel,
        (sds((rows, width), BF), sds((experts, CAP, tiles, LANES), BF)), [SM, SM, VM, VM, VM],
        [pltpu.VMEM((rows * tiles, LANES), F32)],
        nbytes=COST,
    )(expert_ids, slot, summed, residual_in, norm_gain.reshape(1, width))
    arrived = a2a(routed)
    (up_w,) = stage(w_up, after=(attn_proj,))
    ffe = w_gate.shape[2]
    slots_in = n * CAP

    def run_expert(xin, wu, wg, wd):
        return call(
            expert_kernel,
            sds((n, CAP, tiles, LANES), BF), [VM, VM, ANY, ANY],
            [
                pltpu.VMEM((slots_in * tiles, LANES), F32),
                pltpu.VMEM((slots_in, width), BF),
                pltpu.VMEM((slots_in * tiles, LANES), F32),
                pltpu.VMEM((width, ffe), BF),
                pltpu.VMEM((ffe, width), BF),
                pltpu.SemaphoreType.DMA((GATE_PARTS,)),
                pltpu.SemaphoreType.DMA((DOWN_PARTS,)),
            ],
            room=49, flops=6 * slots_in * width * ffe, nbytes=6 * width * ffe,
        )(xin, wu, wg, wd)

    per_device = w_gate.shape[0]
    if per_device == 1:
        done = run_expert(arrived, up_w[0], w_gate[0], w_down[0])
    else:
        split = arrived.reshape(n, per_device, CAP, tiles, LANES)
        done = jnp.stack(
            [run_expert(split[:, e], up_w[e], w_gate[e], w_down[e]) for e in range(per_device)], axis=1
        ).reshape(arrived.shape)
    returned = a2a(done)
    layer_out = call(
        finish_kernel,
        sds((rows, width), BF), [SM, SM, SM, VM, VM, VM],
        [pltpu.VMEM((rows * tiles, LANES), F32)],
        nbytes=1 << 19,
    )(expert_ids, slot, route_weight, returned, residual_in, attn_proj)
    return (attn_proj, layer_out)


def solution(mesh):
    both = P(("groups", "section"), None)
    placed = (
        both,
        P(None, ("groups", "section"), None),
        both,
        P(("groups", "section")),
        both,
        P("section", None),
        P(),
        both,
        both,
        P("section", None, None),
        P("section", None, None),
        P("section", None, None),
    )

    return jax.shard_map(
        shards,
        mesh=mesh,
        in_specs=placed,
        out_specs=(both, both),
        check_vma=False,
    )
```

```python
import functools

import jax
import jax.numpy as jnp
from jax import lax
from jax.experimental import pallas as pl
from jax.experimental.pallas import tpu as pltpu
from jax.sharding import PartitionSpec as P


HEADS = 32
KV_HEADS = 4
WIDTH = 128
CAP = 2
BLOCK_TOKENS = 64
LANES = 128
GROUP = 8
STATS = 8
BATCH = 16
NEG = -1e30
COST = 1 << 26
PROJECT_ROOM = 16
GATE_PARTS = 3
DOWN_PARTS = 4
BF = jnp.bfloat16
F32 = jnp.float32

VM = pl.BlockSpec(memory_space=pltpu.VMEM)
SM = pl.BlockSpec(memory_space=pltpu.SMEM)
HB = pl.BlockSpec(memory_space=pltpu.HBM)
ANY = pl.BlockSpec(memory_space=pl.ANY)


def call(kernel, out_shape, in_specs, scratch, flops=0, nbytes=0, room=8, out=None):
    return pl.pallas_call(
        kernel,
        out_shape=out_shape,
        in_specs=in_specs,
        out_specs=out if out is not None else jax.tree.map(lambda _: VM, out_shape),
        scratch_shapes=scratch,
        compiler_params=pltpu.CompilerParams(vmem_limit_bytes=room << 20),
        cost_estimate=pl.CostEstimate(flops=flops, bytes_accessed=nbytes, transcendentals=0),
    )


def stage_kernel(count, *refs):
    sem = refs[-1]
    outs = refs[-1 - count:-1]
    copies = [pltpu.make_async_copy(refs[i], outs[i], sem.at[i]) for i in range(count)]
    for c in copies:
        c.start()
    for c in copies:
        c.wait()


def stage(*arrays, after=()):
    count = len(arrays)
    nbytes = sum(a.size * a.dtype.itemsize for a in arrays)
    return call(
        functools.partial(stage_kernel, count),
        tuple(jax.ShapeDtypeStruct(a.shape, a.dtype) for a in arrays),
        [ANY] * (count + len(after)), [pltpu.SemaphoreType.DMA((count,))],
        nbytes=nbytes,
    )(*arrays, *after)


def pack_kernel(run, slots, blocks, ids_in, q_in, out, ids, q, qs, meta, sem):
    rows = q.shape[0]
    picks = ids.shape[1]
    get_ids = pltpu.make_async_copy(ids_in, ids, sem.at[0])
    get_q = pltpu.make_async_copy(q_in, q, sem.at[1])
    get_ids.start()
    get_q.start()
    get_q.wait()
    for h in range(HEADS):
        qs[pl.ds(h, rows, stride=HEADS), :] = q[:, h * WIDTH:(h + 1) * WIDTH].astype(F32)
    meta[...] = jnp.zeros_like(meta)
    get_ids.wait()
    if rows * picks != out.shape[0] * slots:
        out[...] = jnp.zeros_like(out)
    lane = lax.broadcasted_iota(jnp.int32, (1, LANES), 1)
    for r in range(rows):
        tile = qs[r * HEADS:(r + 1) * HEADS, :].astype(BF)
        slot = r // run
        for j in range(picks):
            b = ids[r, j]
            dev = lax.div(b, blocks)
            local = b - dev * blocks
            out[dev, slot * HEADS:(slot + 1) * HEADS, :] = tile
            meta[dev, slot:slot + 1, :] = jnp.where(
                lane == 0, local + 1, jnp.where(lane == 1, r % run, 0)
            ).astype(F32)
    out[:, slots * HEADS:, :] = meta[...].astype(BF)


def attend_kernel(n, slots, g, hg, lens_in, x, kv, out, lens, mv, ms, of, mx, sg, ob, sem, so):
    get_lens = pltpu.make_async_copy(lens_in, lens, sem.at[1])
    get_lens.start()
    pairs = n * slots
    per = pairs // g
    cnt = n // g
    ngrp = n // g
    qrows = slots * HEADS
    gw = HEADS // KV_HEADS
    span = hg * per

    sg[...] = x[:, qrows:qrows + 8, :].astype(F32).reshape(n * 8, LANES)
    for q in range(slots):
        mv[q * 8:(q + 1) * 8, 0:n] = jnp.transpose(
            sg[pl.ds(q, n, stride=8), :])[0:8, :].astype(jnp.int32)
    table = pltpu.make_async_copy(mv, ms, sem.at[0])
    table.start()
    table.wait()
    get_lens.wait()
    sg[...] = jnp.zeros_like(sg)
    lane = lax.broadcasted_iota(jnp.int32, (HEADS, LANES), 1)
    column = lax.broadcasted_iota(jnp.int32, (HEADS, KV_HEADS * BLOCK_TOKENS), 1)
    owner = lax.div(lax.broadcasted_iota(jnp.int32, column.shape, 0), gw)
    tok = jnp.where(lax.div(column, BLOCK_TOKENS) == owner, lax.rem(column, BLOCK_TOKENS), BLOCK_TOKENS)

    def some(step, carry):
        todo = []
        for d in range(BATCH):
            dev = step * BATCH + d
            for q in range(slots):
                blk = ms[q * 8, dev] - 1
                safe = jnp.maximum(blk, 0)
                length = jnp.where(blk >= 0, lens[safe], 0)
                base = pl.multiple_of(safe * BLOCK_TOKENS, BLOCK_TOKENS)
                pos = lax.rem(dev, g) * per + q * cnt + lax.div(dev, g)
                todo.append((dev, q, length, base, pos, ms[q * 8 + 1, dev]))
        scores = []
        for dev, q, length, base, pos, rr in todo:
            kb = kv[0, pl.ds(base, BLOCK_TOKENS), :]
            kc = jnp.concatenate([kb[:, k * WIDTH:(k + 1) * WIDTH] for k in range(KV_HEADS)], axis=0)
            scores.append(lax.dot_general(
                x[dev, q * HEADS:(q + 1) * HEADS, :], kc,
                (((1,), (1,)), ((), ())), preferred_element_type=F32))
        soft = []
        for s, (dev, q, length, base, pos, rr) in zip(scores, todo):
            s = jnp.where(tok < length, s * (WIDTH ** -0.5), NEG)
            m = jnp.max(s, axis=-1, keepdims=True)
            w = jnp.where(tok < length, jnp.exp(s - m), 0.0).astype(BF)
            l = jnp.sum(w.astype(F32), axis=-1, keepdims=True)
            soft.append((m, w, l))
        for (m, w, l), (dev, q, length, base, pos, rr) in zip(soft, todo):
            vb = kv[1, pl.ds(base, BLOCK_TOKENS), :]
            vc = jnp.concatenate([vb[:, k * WIDTH:(k + 1) * WIDTH] for k in range(KV_HEADS)], axis=0)
            of[pl.ds(pos, HEADS, stride=pairs), :] = jnp.dot(
                w, vc, preferred_element_type=F32)
        top, tot, who = carry
        for (m, w, l), (dev, q, length, base, pos, rr) in zip(soft, todo):
            here = lane == pos
            top = jnp.where(here, m, top)
            tot = jnp.where(here, l, tot)
            who = jnp.where(here[0:1], rr.astype(F32), who)
        return top, tot, who

    zero = jnp.zeros((HEADS, LANES), F32)
    top, tot, who = lax.fori_loop(0, n // BATCH, some, (zero, zero, zero[0:1]))

    who = jnp.broadcast_to(who, top.shape)
    hi = top.astype(BF).astype(F32)
    mid = (top - hi).astype(BF).astype(F32)
    big = tot.astype(BF).astype(F32)
    copies = LANES // span
    for t, v in enumerate((hi, mid, top - hi - mid, big, tot - big, who)):
        mx[...] = v
        for i in range(g):
            row = jnp.concatenate(
                [mx[pl.ds(hh, ngrp, stride=hg), :][:, i * per:(i + 1) * per] for hh in range(hg)] * copies, axis=1)
            sg[pl.ds(i * STATS + t, ngrp, stride=g * STATS), :] = row
    ob[:, span:, :] = sg[...].reshape(n, STATS, LANES).astype(BF)
    sends = []
    for grp in range(ngrp):
        for hh in range(hg):
            h = grp * hg + hh
            for i in range(g):
                at = h * pairs + i * per
                ob[grp * g + i, hh * per:(hh + 1) * per, :] = of[at:at + per, :].astype(BF)
        sends.append(pltpu.make_async_copy(
            ob.at[pl.ds(grp * g, g)], out.at[pl.ds(grp * g, g)], so.at[grp]))
        sends[-1].start()
    for c in sends:
        c.wait()


def attend(n, slots, g, hg, block_len, asked, key_value_cache):
    pairs = n * slots
    span = hg * (pairs // g)
    sds = jax.ShapeDtypeStruct
    return call(
        functools.partial(attend_kernel, n, slots, g, hg),
        sds((n, span + STATS, LANES), BF), [HB, VM, VM],
        [
            pltpu.SMEM(block_len.shape, jnp.int32),
            pltpu.VMEM((slots * 8, LANES), jnp.int32),
            pltpu.SMEM((slots * 8, LANES), jnp.int32),
            pltpu.VMEM((pairs * HEADS, LANES), F32),
            pltpu.VMEM((HEADS, LANES), F32),
            pltpu.VMEM((n * STATS, LANES), F32),
            pltpu.VMEM((n, span + STATS, LANES), BF),
            pltpu.SemaphoreType.DMA((2,)),
            pltpu.SemaphoreType.DMA((n // g,)),
        ],
        out=ANY, flops=4 * HEADS * pairs * BLOCK_TOKENS * WIDTH, nbytes=COST,
    )(block_len, asked, key_value_cache)


def project_kernel(n, slots, g, hg, run, rows, x, *refs):
    pieces = refs[:g]
    outs = refs[g:g + n // g]
    sf, cm, ws, sp, sem = refs[g + n // g:]
    fw = pieces[0].shape[0]
    me = lax.rem(lax.axis_index("section"), g)
    mine_group = lax.div(lax.axis_index("section"), g)
    loads = []
    for i, piece in enumerate(pieces):
        at = pl.multiple_of(lax.bitwise_xor(me, i) * fw, fw)
        loads.append(pltpu.make_async_copy(piece, ws.at[pl.ds(at, fw)], sem.at[i]))
        loads[-1].start()
    pairs = n * slots
    per = pairs // g
    span = hg * per
    cnt = n // g
    sf[...] = x[:, span:, :].astype(F32).reshape(n * STATS, LANES)
    m = (sf[pl.ds(0, n, stride=STATS), :] + sf[pl.ds(1, n, stride=STATS), :]
         + sf[pl.ds(2, n, stride=STATS), :])
    l = sf[pl.ds(3, n, stride=STATS), :] + sf[pl.ds(4, n, stride=STATS), :]
    rid = sf[pl.ds(5, n, stride=STATS), :]
    peak = jnp.zeros_like(m)
    for r in range(run):
        mine = rid == r
        top = jnp.max(jnp.where(mine, m, -3e38), axis=0, keepdims=True)
        peak = jnp.where(mine, top, peak)
    f = jnp.exp(m - peak)
    fl = f * l
    den = jnp.ones_like(m)
    for r in range(run):
        mine = rid == r
        tot = jnp.sum(jnp.where(mine, fl, 0.0), axis=0, keepdims=True)
        den = jnp.where(mine, tot, den)
    c = f / den
    lane = lax.broadcasted_iota(jnp.int32, (n, LANES), 1)
    inner = lax.rem(lane, span)
    hh = lax.div(inner, per)
    pl_ = lax.rem(inner, per)
    q = lax.div(pl_, cnt)
    s = lax.rem(pl_, cnt)
    local = rows * cnt
    target = hh * local + s * rows + q * run + rid.astype(jnp.int32)
    dpt = LANES // span
    total = hg * local
    row = lax.broadcasted_iota(jnp.int32, (total, LANES), 0)
    side = lax.div(lax.broadcasted_iota(jnp.int32, (1, LANES), 1), span)
    for t in range(n // dpt):
        blk_c = c[t * dpt:t * dpt + 1, :]
        blk_t = target[t * dpt:t * dpt + 1, :]
        for u in range(1, dpt):
            d = t * dpt + u
            blk_c = jnp.where(side == u, c[d:d + 1, :], blk_c)
            blk_t = jnp.where(side == u, target[d:d + 1, :], blk_t)
        cm[:, t * LANES:(t + 1) * LANES] = jnp.where(row == blk_t, blk_c, 0.0).astype(BF)
    a = x[:, 0:span, :].reshape(n * span, LANES)
    att = jnp.dot(cm[...], a, preferred_element_type=F32).astype(BF)
    att = jnp.concatenate([att[i * local:(i + 1) * local, :] for i in range(hg)], axis=1)
    for c in loads:
        c.wait()
    for col in range(0, ws.shape[1], 512):
        p = jnp.dot(att, ws[:, col:col + 512], preferred_element_type=F32)
        for s_ in range(cnt):
            sp[s_, :, col:col + 512] = p[s_ * rows:(s_ + 1) * rows]
    for j, out in enumerate(outs):
        out[...] = sp[lax.bitwise_xor(mine_group, j)].astype(BF)


def norm_kernel(count, eid, slot, *refs):
    x = refs[:count]
    res, gain, proj, out, nf = refs[count:]
    rows, width = res.shape
    acc = x[0][...].astype(F32)
    for i in range(1, count):
        acc = acc + x[i][...].astype(F32)
    p = acc.astype(BF)
    proj[...] = p
    stream = res[...].astype(F32) + p.astype(F32)
    ms = jnp.mean(stream * stream, axis=-1, keepdims=True)
    nrm = stream * lax.rsqrt(ms + 1e-06) * gain[...]
    tiles = width // LANES
    for c in range(tiles):
        nf[pl.ds(c, rows, stride=tiles), :] = nrm[:, c * LANES:(c + 1) * LANES]
    if rows * eid.shape[1] != out.shape[0] * CAP:
        out[...] = jnp.zeros_like(out)
    for r in range(rows):
        tile = nf[r * tiles:(r + 1) * tiles, :].astype(BF)
        for k in range(eid.shape[1]):
            out[eid[r, k], slot[r, k]] = tile


def expert_kernel(x, wu, wg, wd, out, xf, xb, of, gb, db, sg, sd):
    n, cap, tiles, _ = x.shape
    m = n * cap
    width, ffe = wu.shape
    gc = ffe // GATE_PARTS
    dc = width // DOWN_PARTS
    gate = [pltpu.make_async_copy(
        wg.at[:, pl.ds(i * gc, gc)], gb.at[:, pl.ds(i * gc, gc)], sg.at[i]) for i in range(GATE_PARTS)]
    down = [pltpu.make_async_copy(
        wd.at[:, pl.ds(i * dc, dc)], db.at[:, pl.ds(i * dc, dc)], sd.at[i]) for i in range(DOWN_PARTS)]
    for c in gate + down:
        c.start()
    xf[...] = x[...].astype(F32).reshape(m * tiles, LANES)
    for c in range(tiles):
        xb[:, c * LANES:(c + 1) * LANES] = xf[pl.ds(c, m, stride=tiles), :].astype(BF)
    ua = jnp.dot(xb[...], wu[...], preferred_element_type=F32)
    parts = []
    for i, c in enumerate(gate):
        c.wait()
        ga = jnp.dot(xb[...], gb[:, i * gc:(i + 1) * gc], preferred_element_type=F32)
        parts.append((ga / (1.0 + jnp.exp(-ga)) * ua[:, i * gc:(i + 1) * gc]).astype(BF))
    h = jnp.concatenate(parts, axis=1)
    for i, c in enumerate(down):
        c.wait()
        o = jnp.dot(h, db[:, i * dc:(i + 1) * dc], preferred_element_type=F32)
        for t in range(dc // LANES):
            of[pl.ds(i * dc // LANES + t, m, stride=tiles), :] = o[:, t * LANES:(t + 1) * LANES]
    out[...] = of[...].astype(BF).reshape(n, cap, tiles, LANES)


def finish_kernel(eid, slot, rw, x, res, proj, out, acc):
    rows, width = res.shape
    tiles = width // LANES
    for r in range(rows):
        a = jnp.zeros((tiles, LANES), F32)
        for k in range(eid.shape[1]):
            a = a + rw[r, k] * x[eid[r, k], slot[r, k]].astype(F32)
        acc[r * tiles:(r + 1) * tiles, :] = a
    for c in range(tiles):
        sl = slice(c * LANES, (c + 1) * LANES)
        stream = res[:, sl].astype(F32) + proj[:, sl].astype(F32)
        out[:, sl] = (stream + acc[pl.ds(c, rows, stride=tiles), :]).astype(BF)


def shards(
    queries,
    key_value_cache,
    block_ids,
    block_len,
    residual_in,
    out_weight,
    norm_gain,
    expert_ids,
    route_weight,
    w_gate,
    w_up,
    w_down,
):
    n = lax.axis_size("section")
    rows, _ = queries.shape
    picks = block_ids.shape[1]
    blocks = block_len.shape[0]
    width = residual_in.shape[1]
    run = n // picks
    slots = (rows + run - 1) // run
    g = GROUP
    fw = out_weight.shape[0]
    hg = g * fw // WIDTH
    pairs = n * slots
    per = pairs // g
    span = hg * per
    cnt = n // g
    tiles = width // LANES
    a2a = functools.partial(
        lax.all_to_all, axis_name="section", split_axis=0, concat_axis=0, tiled=True)
    sds = jax.ShapeDtypeStruct

    pieces = [None] * g
    for far in range(0, g, 2):
        if far:
            pieces[far] = lax.ppermute(out_weight, "section", [(i, i ^ far) for i in range(n)])
        else:
            pieces[0] = out_weight
    for far in range(0, g, 2):
        pieces[far + 1] = lax.ppermute(pieces[far], "section", [(i, i ^ 1) for i in range(n)])
    (cache,) = stage(key_value_cache)
    flat = expert_ids.reshape(-1)
    place = jnp.arange(flat.shape[0])
    slot = jnp.sum(
        (flat[:, None] == flat[None, :]) & (place[:, None] > place[None, :]), axis=1
    ).astype(jnp.int32).reshape(expert_ids.shape)

    chunk = slots * HEADS + 8
    sent = call(
        functools.partial(pack_kernel, run, slots, blocks),
        sds((n, chunk, LANES), BF), [HB, HB],
        [
            pltpu.SMEM(block_ids.shape, jnp.int32),
            pltpu.VMEM(queries.shape, BF),
            pltpu.VMEM((rows * HEADS, LANES), F32),
            pltpu.VMEM((n, 8, LANES), F32),
            pltpu.SemaphoreType.DMA((2,)),
        ],
        nbytes=COST, room=60,
    )(block_ids, queries)
    asked = a2a(sent)
    parts = attend(n, slots, g, hg, block_len, asked, cache)
    back = a2a(parts)
    local = rows * cnt
    partial = call(
        functools.partial(project_kernel, n, slots, g, hg, run, rows),
        (sds((rows, width), BF),) * cnt, [VM] + [ANY] * g,
        [
            pltpu.VMEM((n * STATS, LANES), F32),
            pltpu.VMEM((hg * local, n * span), BF),
            pltpu.VMEM((g * fw, width), BF),
            pltpu.VMEM((cnt, rows, width), F32),
            pltpu.SemaphoreType.DMA((g,)),
        ],
        flops=2 * local * g * fw * width, nbytes=COST, room=PROJECT_ROOM,
    )(back, *pieces)
    summed = [partial[0]]
    for j in range(1, cnt):
        summed.append(lax.ppermute(partial[j], "section", [(i, i ^ (j * g)) for i in range(n)]))
    experts = n * w_gate.shape[0]
    attn_proj, routed = call(
        functools.partial(norm_kernel, cnt),
        (sds((rows, width), BF), sds((experts, CAP, tiles, LANES), BF)), [SM, SM] + [VM] * (cnt + 2),
        [pltpu.VMEM((rows * tiles, LANES), F32)],
        nbytes=COST,
    )(expert_ids, slot, *summed, residual_in, norm_gain.reshape(1, width))
    arrived = a2a(routed)
    (up_w,) = stage(w_up, after=(attn_proj,))
    ffe = w_gate.shape[2]
    slots_in = n * CAP

    def run_expert(xin, wu, wg, wd):
        return call(
            expert_kernel,
            sds((n, CAP, tiles, LANES), BF), [VM, VM, ANY, ANY],
            [
                pltpu.VMEM((slots_in * tiles, LANES), F32),
                pltpu.VMEM((slots_in, width), BF),
                pltpu.VMEM((slots_in * tiles, LANES), F32),
                pltpu.VMEM((width, ffe), BF),
                pltpu.VMEM((ffe, width), BF),
                pltpu.SemaphoreType.DMA((GATE_PARTS,)),
                pltpu.SemaphoreType.DMA((DOWN_PARTS,)),
            ],
            room=49, flops=6 * slots_in * width * ffe, nbytes=6 * width * ffe,
        )(xin, wu, wg, wd)

    per_device = w_gate.shape[0]
    if per_device == 1:
        done = run_expert(arrived, up_w[0], w_gate[0], w_down[0])
    else:
        split = arrived.reshape(n, per_device, CAP, tiles, LANES)
        done = jnp.stack(
            [run_expert(split[:, e], up_w[e], w_gate[e], w_down[e]) for e in range(per_device)], axis=1
        ).reshape(arrived.shape)
    returned = a2a(done)
    layer_out = call(
        finish_kernel,
        sds((rows, width), BF), [SM, SM, SM, VM, VM, VM],
        [pltpu.VMEM((rows * tiles, LANES), F32)],
        nbytes=1 << 19,
    )(expert_ids, slot, route_weight, returned, residual_in, attn_proj)
    return (attn_proj, layer_out)


def solution(mesh):
    both = P(("groups", "section"), None)
    placed = (
        both,
        P(None, ("groups", "section"), None),
        both,
        P(("groups", "section")),
        both,
        P("section", None),
        P(),
        both,
        both,
        P("section", None, None),
        P("section", None, None),
        P("section", None, None),
    )

    return jax.shard_map(
        shards,
        mesh=mesh,
        in_specs=placed,
        out_specs=(both, both),
        check_vma=False,
    )
```

```python
import functools

import jax
import jax.numpy as jnp
from jax import lax
from jax.experimental import pallas as pl
from jax.experimental.pallas import tpu as pltpu
from jax.sharding import PartitionSpec as P


HEADS = 32
KV_HEADS = 4
WIDTH = 128
CAP = 2
BLOCK_TOKENS = 64
LANES = 128
GROUP = 8
STATS = 8
CLASSES = 4
NEG = -1e30
COST = 1 << 26
PROJECT_ROOM = 16
GATE_PARTS = 3
DOWN_PARTS = 4
BF = jnp.bfloat16
F32 = jnp.float32

VM = pl.BlockSpec(memory_space=pltpu.VMEM)
SM = pl.BlockSpec(memory_space=pltpu.SMEM)
HB = pl.BlockSpec(memory_space=pltpu.HBM)
ANY = pl.BlockSpec(memory_space=pl.ANY)


def call(kernel, out_shape, in_specs, scratch, flops=0, nbytes=0, room=8, out=None):
    return pl.pallas_call(
        kernel,
        out_shape=out_shape,
        in_specs=in_specs,
        out_specs=out if out is not None else jax.tree.map(lambda _: VM, out_shape),
        scratch_shapes=scratch,
        compiler_params=pltpu.CompilerParams(vmem_limit_bytes=room << 20),
        cost_estimate=pl.CostEstimate(flops=flops, bytes_accessed=nbytes, transcendentals=0),
    )


def stage_kernel(count, *refs):
    sem = refs[-1]
    outs = refs[-1 - count:-1]
    copies = [pltpu.make_async_copy(refs[i], outs[i], sem.at[i]) for i in range(count)]
    for c in copies:
        c.start()
    for c in copies:
        c.wait()


def stage(*arrays, after=()):
    count = len(arrays)
    nbytes = sum(a.size * a.dtype.itemsize for a in arrays)
    return call(
        functools.partial(stage_kernel, count),
        tuple(jax.ShapeDtypeStruct(a.shape, a.dtype) for a in arrays),
        [ANY] * (count + len(after)), [pltpu.SemaphoreType.DMA((count,))],
        nbytes=nbytes,
    )(*arrays, *after)


def pack_kernel(run, slots, blocks, ids_in, q_in, out, ids, q, qs, meta, sem):
    rows = q.shape[0]
    picks = ids.shape[1]
    get_ids = pltpu.make_async_copy(ids_in, ids, sem.at[0])
    get_q = pltpu.make_async_copy(q_in, q, sem.at[1])
    get_ids.start()
    get_q.start()
    get_q.wait()
    for h in range(HEADS):
        qs[pl.ds(h, rows, stride=HEADS), :] = q[:, h * WIDTH:(h + 1) * WIDTH].astype(F32)
    meta[...] = jnp.zeros_like(meta)
    get_ids.wait()
    if rows * picks != out.shape[0] * slots:
        out[...] = jnp.zeros_like(out)
    lane = lax.broadcasted_iota(jnp.int32, (1, LANES), 1)
    for r in range(rows):
        tile = qs[r * HEADS:(r + 1) * HEADS, :].astype(BF)
        slot = r // run
        for j in range(picks):
            b = ids[r, j]
            dev = lax.div(b, blocks)
            local = b - dev * blocks
            out[dev, slot * HEADS:(slot + 1) * HEADS, :] = tile
            meta[dev, slot:slot + 1, :] = jnp.where(
                lane == 0, local + 1, jnp.where(lane == 1, r % run, 0)
            ).astype(F32)
    out[:, slots * HEADS:, :] = meta[...].astype(BF)


def attend_kernel(n, slots, g, hg, lens_in, x, kv, out, lens, mv, ms, sg, ob, sem, so, st):
    get_lens = pltpu.make_async_copy(lens_in, lens, sem.at[1])
    get_lens.start()
    cnt = n // g
    ngrp = n // g
    per = slots * cnt
    qrows = slots * HEADS
    gw = HEADS // KV_HEADS
    span = hg * per

    sg[...] = x[:, qrows:qrows + 8, :].astype(F32).reshape(n * 8, LANES)
    for q in range(slots):
        mv[q * 8:(q + 1) * 8, 0:n] = jnp.transpose(
            sg[pl.ds(q, n, stride=8), :])[0:8, :].astype(jnp.int32)
    table = pltpu.make_async_copy(mv, ms, sem.at[0])
    table.start()
    sg[...] = jnp.zeros_like(sg)
    lane = lax.broadcasted_iota(jnp.int32, (HEADS, LANES), 1)
    spot = lax.rem(lax.div(lane, hg), per)
    own = lax.rem(lane, hg) == lax.rem(lax.broadcasted_iota(jnp.int32, lane.shape, 0), hg)
    column = lax.broadcasted_iota(jnp.int32, (HEADS, KV_HEADS * BLOCK_TOKENS), 1)
    owner = lax.div(lax.broadcasted_iota(jnp.int32, column.shape, 0), gw)
    tok = jnp.where(lax.div(column, BLOCK_TOKENS) == owner, lax.rem(column, BLOCK_TOKENS), BLOCK_TOKENS)
    table.wait()
    get_lens.wait()

    def send(step, grp):
        first = grp * g + step * CLASSES
        return pltpu.make_async_copy(
            ob.at[pl.ds(first, CLASSES), 0:span], out.at[pl.ds(first, CLASSES), 0:span], so.at[step, grp])

    def lump(v):
        v = jnp.where(own, v, 0.0)
        return jnp.concatenate(
            [jnp.sum(v[a:a + hg], axis=0, keepdims=True) for a in range(0, HEADS, hg)], axis=0)

    def some(step, carry):
        todo = []
        for c in range(CLASSES):
            i = step * CLASSES + c
            for q in range(slots):
                for s in range(cnt):
                    dev = s * g + i
                    blk = ms[q * 8, dev] - 1
                    safe = jnp.maximum(blk, 0)
                    length = jnp.where(blk >= 0, lens[safe], 0)
                    base = pl.multiple_of(safe * BLOCK_TOKENS, BLOCK_TOKENS)
                    todo.append((dev, q, length, base, c, q * cnt + s, ms[q * 8 + 1, dev]))
        scores = []
        for dev, q, length, base, c, at, rr in todo:
            kb = kv[0, pl.ds(base, BLOCK_TOKENS), :]
            kc = jnp.concatenate([kb[:, k * WIDTH:(k + 1) * WIDTH] for k in range(KV_HEADS)], axis=0)
            scores.append(lax.dot_general(
                x[dev, q * HEADS:(q + 1) * HEADS, :], kc,
                (((1,), (1,)), ((), ())), preferred_element_type=F32))
        soft = []
        for s, (dev, q, length, base, c, at, rr) in zip(scores, todo):
            s = jnp.where(tok < length, s * (WIDTH ** -0.5), NEG)
            m = jnp.max(s, axis=-1, keepdims=True)
            w = jnp.where(tok < length, jnp.exp(s - m), 0.0).astype(BF)
            l = jnp.sum(w.astype(F32), axis=-1, keepdims=True)
            soft.append((m, w, l))
        for (m, w, l), (dev, q, length, base, c, at, rr) in zip(soft, todo):
            vb = kv[1, pl.ds(base, BLOCK_TOKENS), :]
            vc = jnp.concatenate([vb[:, k * WIDTH:(k + 1) * WIDTH] for k in range(KV_HEADS)], axis=0)
            o = jnp.dot(w, vc, preferred_element_type=F32)
            for grp in range(ngrp):
                ob[grp * g + step * CLASSES + c, at * hg:(at + 1) * hg, :] = o[grp * hg:(grp + 1) * hg].astype(BF)
        for grp in range(ngrp):
            send(step, grp).start()
        for c in range(CLASSES):
            top = jnp.zeros((HEADS, LANES), F32)
            tot = jnp.zeros((HEADS, LANES), F32)
            who = jnp.zeros((1, LANES), F32)
            for (m, w, l), (dev, q, length, base, cc, at, rr) in zip(soft, todo):
                if cc == c:
                    here = spot == at
                    top = jnp.where(here, m, top)
                    tot = jnp.where(here, l, tot)
                    who = jnp.where(here[0:1], rr.astype(F32), who)
            top = lump(top)
            tot = lump(tot)
            hi = top.astype(BF).astype(F32)
            mid = (top - hi).astype(BF).astype(F32)
            big = tot.astype(BF).astype(F32)
            for t, v in enumerate((hi, mid, top - hi - mid, big, tot - big, jnp.broadcast_to(who, top.shape))):
                sg[pl.ds((step * CLASSES + c) * STATS + t, ngrp, stride=g * STATS), :] = v
        return carry

    steps = g // CLASSES
    lax.fori_loop(0, steps, some, 0)
    ob[:, span:, :] = sg[...].reshape(n, STATS, LANES).astype(BF)
    last = pltpu.make_async_copy(ob.at[:, span:], out.at[:, span:], st)
    last.start()
    for step in range(steps):
        for grp in range(ngrp):
            send(step, grp).wait()
    last.wait()


def attend(n, slots, g, hg, block_len, asked, key_value_cache):
    pairs = n * slots
    span = hg * (pairs // g)
    sds = jax.ShapeDtypeStruct
    return call(
        functools.partial(attend_kernel, n, slots, g, hg),
        sds((n, span + STATS, LANES), BF), [HB, VM, VM],
        [
            pltpu.SMEM(block_len.shape, jnp.int32),
            pltpu.VMEM((slots * 8, LANES), jnp.int32),
            pltpu.SMEM((slots * 8, LANES), jnp.int32),
            pltpu.VMEM((n * STATS, LANES), F32),
            pltpu.VMEM((n, span + STATS, LANES), BF),
            pltpu.SemaphoreType.DMA((2,)),
            pltpu.SemaphoreType.DMA((g // CLASSES, n // g)),
            pltpu.SemaphoreType.DMA,
        ],
        out=ANY, flops=4 * HEADS * pairs * BLOCK_TOKENS * WIDTH, nbytes=COST,
    )(block_len, asked, key_value_cache)


def project_kernel(n, slots, g, hg, run, rows, x, *refs):
    pieces = refs[:g]
    outs = refs[g:g + n // g]
    sf, cm, ws, sp, sem = refs[g + n // g:]
    fw = pieces[0].shape[0]
    me = lax.rem(lax.axis_index("section"), g)
    mine_group = lax.div(lax.axis_index("section"), g)
    loads = []
    for i, piece in enumerate(pieces):
        at = pl.multiple_of(lax.bitwise_xor(me, i) * fw, fw)
        loads.append(pltpu.make_async_copy(piece, ws.at[pl.ds(at, fw)], sem.at[i]))
        loads[-1].start()
    pairs = n * slots
    per = pairs // g
    span = hg * per
    cnt = n // g
    sf[...] = x[:, span:, :].astype(F32).reshape(n * STATS, LANES)
    m = (sf[pl.ds(0, n, stride=STATS), :] + sf[pl.ds(1, n, stride=STATS), :]
         + sf[pl.ds(2, n, stride=STATS), :])
    l = sf[pl.ds(3, n, stride=STATS), :] + sf[pl.ds(4, n, stride=STATS), :]
    rid = sf[pl.ds(5, n, stride=STATS), :]
    peak = jnp.zeros_like(m)
    for r in range(run):
        mine = rid == r
        top = jnp.max(jnp.where(mine, m, -3e38), axis=0, keepdims=True)
        peak = jnp.where(mine, top, peak)
    f = jnp.exp(m - peak)
    fl = f * l
    den = jnp.ones_like(m)
    for r in range(run):
        mine = rid == r
        tot = jnp.sum(jnp.where(mine, fl, 0.0), axis=0, keepdims=True)
        den = jnp.where(mine, tot, den)
    c = f / den
    lane = lax.broadcasted_iota(jnp.int32, (n, LANES), 1)
    inner = lax.rem(lane, span)
    hh = lax.rem(inner, hg)
    pl_ = lax.div(inner, hg)
    q = lax.div(pl_, cnt)
    s = lax.rem(pl_, cnt)
    local = rows * cnt
    target = hh * local + s * rows + q * run + rid.astype(jnp.int32)
    dpt = LANES // span
    total = hg * local
    row = lax.broadcasted_iota(jnp.int32, (total, LANES), 0)
    side = lax.div(lax.broadcasted_iota(jnp.int32, (1, LANES), 1), span)
    for t in range(n // dpt):
        blk_c = c[t * dpt:t * dpt + 1, :]
        blk_t = target[t * dpt:t * dpt + 1, :]
        for u in range(1, dpt):
            d = t * dpt + u
            blk_c = jnp.where(side == u, c[d:d + 1, :], blk_c)
            blk_t = jnp.where(side == u, target[d:d + 1, :], blk_t)
        cm[:, t * LANES:(t + 1) * LANES] = jnp.where(row == blk_t, blk_c, 0.0).astype(BF)
    a = x[:, 0:span, :].reshape(n * span, LANES)
    att = jnp.dot(cm[...], a, preferred_element_type=F32).astype(BF)
    att = jnp.concatenate([att[i * local:(i + 1) * local, :] for i in range(hg)], axis=1)
    for c in loads:
        c.wait()
    for col in range(0, ws.shape[1], 512):
        p = jnp.dot(att, ws[:, col:col + 512], preferred_element_type=F32)
        for s_ in range(cnt):
            sp[s_, :, col:col + 512] = p[s_ * rows:(s_ + 1) * rows]
    for j, out in enumerate(outs):
        out[...] = sp[lax.bitwise_xor(mine_group, j)].astype(BF)


def norm_kernel(count, index, *refs):
    x = refs[:count]
    res, gain, proj, out, nf = refs[count:]
    rows, width = res.shape
    acc = x[0][...].astype(F32)
    for i in range(1, count):
        acc = acc + x[i][...].astype(F32)
    p = acc.astype(BF)
    proj[...] = p
    stream = res[...].astype(F32) + p.astype(F32)
    ms = jnp.mean(stream * stream, axis=-1, keepdims=True)
    nrm = stream * lax.rsqrt(ms + 1e-06) * gain[...]
    tiles = width // LANES
    for c in range(tiles):
        nf[pl.ds(c, rows, stride=tiles), :] = nrm[:, c * LANES:(c + 1) * LANES]
    if rows * index.shape[1] != out.shape[0]:
        out[...] = jnp.zeros_like(out)
    for r in range(rows):
        tile = nf[r * tiles:(r + 1) * tiles, :].astype(BF)
        for k in range(index.shape[1]):
            out[index[r, k]] = tile


def expert_kernel(x, wu, wg, wd, out, xf, xb, of, gb, db, sg, sd):
    m, tiles, _ = x.shape
    width, ffe = wu.shape
    gc = ffe // GATE_PARTS
    dc = width // DOWN_PARTS
    gate = [pltpu.make_async_copy(
        wg.at[:, pl.ds(i * gc, gc)], gb.at[:, pl.ds(i * gc, gc)], sg.at[i]) for i in range(GATE_PARTS)]
    down = [pltpu.make_async_copy(
        wd.at[:, pl.ds(i * dc, dc)], db.at[:, pl.ds(i * dc, dc)], sd.at[i]) for i in range(DOWN_PARTS)]
    for c in gate + down:
        c.start()
    xf[...] = x[...].astype(F32).reshape(m * tiles, LANES)
    for c in range(tiles):
        xb[:, c * LANES:(c + 1) * LANES] = xf[pl.ds(c, m, stride=tiles), :].astype(BF)
    ua = jnp.dot(xb[...], wu[...], preferred_element_type=F32)
    parts = []
    for i, c in enumerate(gate):
        c.wait()
        ga = jnp.dot(xb[...], gb[:, i * gc:(i + 1) * gc], preferred_element_type=F32)
        parts.append((ga / (1.0 + jnp.exp(-ga)) * ua[:, i * gc:(i + 1) * gc]).astype(BF))
    h = jnp.concatenate(parts, axis=1)
    for i, c in enumerate(down):
        c.wait()
        o = jnp.dot(h, db[:, i * dc:(i + 1) * dc], preferred_element_type=F32)
        for t in range(dc // LANES):
            of[pl.ds(i * dc // LANES + t, m, stride=tiles), :] = o[:, t * LANES:(t + 1) * LANES]
    out[...] = of[...].astype(BF).reshape(m, tiles, LANES)


def finish_kernel(index, rw, x, res, proj, out, acc):
    rows, width = res.shape
    tiles = width // LANES
    for r in range(rows):
        a = jnp.zeros((tiles, LANES), F32)
        for k in range(index.shape[1]):
            a = a + rw[r, k] * x[index[r, k]].astype(F32)
        acc[r * tiles:(r + 1) * tiles, :] = a
    for c in range(tiles):
        sl = slice(c * LANES, (c + 1) * LANES)
        stream = res[:, sl].astype(F32) + proj[:, sl].astype(F32)
        out[:, sl] = (stream + acc[pl.ds(c, rows, stride=tiles), :]).astype(BF)


def shards(
    queries,
    key_value_cache,
    block_ids,
    block_len,
    residual_in,
    out_weight,
    norm_gain,
    expert_ids,
    route_weight,
    w_gate,
    w_up,
    w_down,
):
    n = lax.axis_size("section")
    rows, _ = queries.shape
    picks = block_ids.shape[1]
    blocks = block_len.shape[0]
    width = residual_in.shape[1]
    run = n // picks
    slots = (rows + run - 1) // run
    g = GROUP
    fw = out_weight.shape[0]
    hg = g * fw // WIDTH
    pairs = n * slots
    per = pairs // g
    span = hg * per
    cnt = n // g
    tiles = width // LANES
    a2a = functools.partial(
        lax.all_to_all, axis_name="section", split_axis=0, concat_axis=0, tiled=True)
    sds = jax.ShapeDtypeStruct

    pieces = [None] * g
    for far in range(0, g, 2):
        if far:
            pieces[far] = lax.ppermute(out_weight, "section", [(i, i ^ far) for i in range(n)])
        else:
            pieces[0] = out_weight
    for far in range(0, g, 2):
        pieces[far + 1] = lax.ppermute(pieces[far], "section", [(i, i ^ 1) for i in range(n)])
    (cache,) = stage(key_value_cache)
    flat = expert_ids.reshape(-1)
    place = jnp.arange(flat.shape[0])
    slot = jnp.sum(
        (flat[:, None] == flat[None, :]) & (place[:, None] > place[None, :]), axis=1
    ).astype(jnp.int32)
    index = (flat * CAP + slot).reshape(expert_ids.shape)

    chunk = slots * HEADS + 8
    sent = call(
        functools.partial(pack_kernel, run, slots, blocks),
        sds((n, chunk, LANES), BF), [HB, HB],
        [
            pltpu.SMEM(block_ids.shape, jnp.int32),
            pltpu.VMEM(queries.shape, BF),
            pltpu.VMEM((rows * HEADS, LANES), F32),
            pltpu.VMEM((n, 8, LANES), F32),
            pltpu.SemaphoreType.DMA((2,)),
        ],
        nbytes=COST, room=60,
    )(block_ids, queries)
    asked = a2a(sent)
    parts = attend(n, slots, g, hg, block_len, asked, cache)
    back = a2a(parts)
    local = rows * cnt
    partial = call(
        functools.partial(project_kernel, n, slots, g, hg, run, rows),
        (sds((rows, width), BF),) * cnt, [VM] + [ANY] * g,
        [
            pltpu.VMEM((n * STATS, LANES), F32),
            pltpu.VMEM((hg * local, n * span), BF),
            pltpu.VMEM((g * fw, width), BF),
            pltpu.VMEM((cnt, rows, width), F32),
            pltpu.SemaphoreType.DMA((g,)),
        ],
        flops=2 * local * g * fw * width, nbytes=COST, room=PROJECT_ROOM,
    )(back, *pieces)
    (up_w,) = stage(w_up, after=(partial[0],))
    summed = [partial[0]]
    for j in range(cnt - 1, 0, -1):
        summed.append(lax.ppermute(partial[j], "section", [(i, i ^ (j * g)) for i in range(n)]))
    experts = n * w_gate.shape[0]
    attn_proj, routed = call(
        functools.partial(norm_kernel, cnt),
        (sds((rows, width), BF), sds((experts * CAP, tiles, LANES), BF)), [SM] + [VM] * (cnt + 2),
        [pltpu.VMEM((rows * tiles, LANES), F32)],
        nbytes=COST,
    )(index, *summed, residual_in, norm_gain.reshape(1, width))
    arrived = a2a(routed)
    ffe = w_gate.shape[2]
    slots_in = n * CAP

    def run_expert(xin, wu, wg, wd):
        return call(
            expert_kernel,
            sds((slots_in, tiles, LANES), BF), [VM, VM, ANY, ANY],
            [
                pltpu.VMEM((slots_in * tiles, LANES), F32),
                pltpu.VMEM((slots_in, width), BF),
                pltpu.VMEM((slots_in * tiles, LANES), F32),
                pltpu.VMEM((width, ffe), BF),
                pltpu.VMEM((ffe, width), BF),
                pltpu.SemaphoreType.DMA((GATE_PARTS,)),
                pltpu.SemaphoreType.DMA((DOWN_PARTS,)),
            ],
            room=49, flops=6 * slots_in * width * ffe, nbytes=6 * width * ffe,
        )(xin, wu, wg, wd)

    per_device = w_gate.shape[0]
    if per_device == 1:
        done = run_expert(arrived, up_w[0], w_gate[0], w_down[0])
    else:
        split = arrived.reshape(n, per_device, CAP, tiles, LANES)
        done = jnp.stack([
            run_expert(split[:, e].reshape(slots_in, tiles, LANES), up_w[e], w_gate[e], w_down[e])
            .reshape(n, CAP, tiles, LANES) for e in range(per_device)], axis=1).reshape(arrived.shape)
    returned = a2a(done)
    layer_out = call(
        finish_kernel,
        sds((rows, width), BF), [SM, SM, VM, VM, VM],
        [pltpu.VMEM((rows * tiles, LANES), F32)],
        nbytes=1 << 19,
    )(index, route_weight, returned, residual_in, attn_proj)
    return (attn_proj, layer_out)


def solution(mesh):
    both = P(("groups", "section"), None)
    placed = (
        both,
        P(None, ("groups", "section"), None),
        both,
        P(("groups", "section")),
        both,
        P("section", None),
        P(),
        both,
        both,
        P("section", None, None),
        P("section", None, None),
        P("section", None, None),
    )

    return jax.shard_map(
        shards,
        mesh=mesh,
        in_specs=placed,
        out_specs=(both, both),
        check_vma=False,
    )
```

```python
import functools

import jax
import jax.numpy as jnp
from jax import lax
from jax.experimental import pallas as pl
from jax.experimental.pallas import tpu as pltpu
from jax.sharding import PartitionSpec as P


HEADS = 32
KV_HEADS = 4
WIDTH = 128
CAP = 2
BLOCK_TOKENS = 64
LANES = 128
GROUP = 8
STATS = 8
CLASSES = 4
NEG = -1e30
COST = 1 << 26
PROJECT_ROOM = 16
GATE_PARTS = 3
DOWN_PARTS = 4
BF = jnp.bfloat16
F32 = jnp.float32

VM = pl.BlockSpec(memory_space=pltpu.VMEM)
SM = pl.BlockSpec(memory_space=pltpu.SMEM)
HB = pl.BlockSpec(memory_space=pltpu.HBM)
ANY = pl.BlockSpec(memory_space=pl.ANY)


def call(kernel, out_shape, in_specs, scratch, flops=0, nbytes=0, room=8, out=None):
    return pl.pallas_call(
        kernel,
        out_shape=out_shape,
        in_specs=in_specs,
        out_specs=out if out is not None else jax.tree.map(lambda _: VM, out_shape),
        scratch_shapes=scratch,
        compiler_params=pltpu.CompilerParams(vmem_limit_bytes=room << 20),
        cost_estimate=pl.CostEstimate(flops=flops, bytes_accessed=nbytes, transcendentals=0),
    )


def stage_kernel(count, *refs):
    sem = refs[-1]
    outs = refs[-1 - count:-1]
    copies = [pltpu.make_async_copy(refs[i], outs[i], sem.at[i]) for i in range(count)]
    for c in copies:
        c.start()
    for c in copies:
        c.wait()


def stage(*arrays, after=()):
    count = len(arrays)
    nbytes = sum(a.size * a.dtype.itemsize for a in arrays)
    return call(
        functools.partial(stage_kernel, count),
        tuple(jax.ShapeDtypeStruct(a.shape, a.dtype) for a in arrays),
        [ANY] * (count + len(after)), [pltpu.SemaphoreType.DMA((count,))],
        nbytes=nbytes,
    )(*arrays, *after)


def pack_kernel(run, slots, blocks, ids_in, q_in, out, ids, q, qs, meta, ob, sem, so):
    rows = q.shape[0]
    picks = ids.shape[1]
    get_ids = pltpu.make_async_copy(ids_in, ids, sem.at[0])
    get_q = pltpu.make_async_copy(q_in, q, sem.at[1])
    get_ids.start()
    get_q.start()
    meta[...] = jnp.zeros_like(meta)
    if rows * picks != out.shape[0] * slots:
        ob[...] = jnp.zeros_like(ob)
    get_q.wait()
    for h in range(HEADS):
        qs[pl.ds(h, rows, stride=HEADS), :] = q[:, h * WIDTH:(h + 1) * WIDTH].astype(F32)
    get_ids.wait()
    lane = lax.broadcasted_iota(jnp.int32, (1, LANES), 1)
    sends = []
    for r in range(rows):
        tile = qs[r * HEADS:(r + 1) * HEADS, :].astype(BF)
        slot = r // run
        for j in range(picks):
            b = ids[r, j]
            dev = lax.div(b, blocks)
            local = b - dev * blocks
            ob[dev, slot * HEADS:(slot + 1) * HEADS, :] = tile
            meta[dev, slot:slot + 1, :] = jnp.where(
                lane == 0, local + 1, jnp.where(lane == 1, r % run, 0)
            ).astype(F32)
        if r % run == run - 1 or r == rows - 1:
            if r == rows - 1:
                ob[:, slots * HEADS:, :] = meta[...].astype(BF)
                part = slice(slot * HEADS, slots * HEADS + 8)
            else:
                part = slice(slot * HEADS, (slot + 1) * HEADS)
            sends.append(pltpu.make_async_copy(ob.at[:, part], out.at[:, part], so.at[slot]))
            sends[-1].start()
    for c in sends:
        c.wait()


def attend_kernel(n, slots, g, hg, lens_in, x, kv, out, lens, mv, ms, sg, ob, sem, so, st):
    get_lens = pltpu.make_async_copy(lens_in, lens, sem.at[1])
    get_lens.start()
    cnt = n // g
    ngrp = n // g
    per = slots * cnt
    qrows = slots * HEADS
    gw = HEADS // KV_HEADS
    span = hg * per

    sg[...] = x[:, qrows:qrows + 8, :].astype(F32).reshape(n * 8, LANES)
    for q in range(slots):
        mv[q * 8:(q + 1) * 8, 0:n] = jnp.transpose(
            sg[pl.ds(q, n, stride=8), :])[0:8, :].astype(jnp.int32)
    table = pltpu.make_async_copy(mv, ms, sem.at[0])
    table.start()
    sg[...] = jnp.zeros_like(sg)
    lane = lax.broadcasted_iota(jnp.int32, (HEADS, LANES), 1)
    spot = lax.rem(lax.div(lane, hg), per)
    own = lax.rem(lane, hg) == lax.rem(lax.broadcasted_iota(jnp.int32, lane.shape, 0), hg)
    held = LANES // BLOCK_TOKENS
    owner = lax.rem(lax.div(lax.broadcasted_iota(jnp.int32, lane.shape, 0), gw), held)
    tok = jnp.where(lax.div(lane, BLOCK_TOKENS) == owner, lax.rem(lane, BLOCK_TOKENS), BLOCK_TOKENS)
    blank = jnp.zeros((held * gw, LANES), BF)
    table.wait()
    get_lens.wait()

    def send(step, grp):
        first = grp * g + step * CLASSES
        return pltpu.make_async_copy(
            ob.at[pl.ds(first, CLASSES), 0:span], out.at[pl.ds(first, CLASSES), 0:span], so.at[step, grp])

    def lump(v):
        v = jnp.where(own, v, 0.0)
        return jnp.concatenate(
            [jnp.sum(v[a:a + hg], axis=0, keepdims=True) for a in range(0, HEADS, hg)], axis=0)

    def some(step, carry):
        todo = []
        for c in range(CLASSES):
            i = step * CLASSES + c
            for q in range(slots):
                for s in range(cnt):
                    dev = s * g + i
                    blk = ms[q * 8, dev] - 1
                    safe = jnp.maximum(blk, 0)
                    length = jnp.where(blk >= 0, lens[safe], 0)
                    base = pl.multiple_of(safe * BLOCK_TOKENS, BLOCK_TOKENS)
                    todo.append((dev, q, length, base, c, q * cnt + s, ms[q * 8 + 1, dev]))
        scores = []
        for dev, q, length, base, c, at, rr in todo:
            kb = kv[0, pl.ds(base, BLOCK_TOKENS), :]
            kc = jnp.concatenate([kb[:, k * WIDTH:(k + 1) * WIDTH] for k in range(KV_HEADS)], axis=0)
            scores.append(lax.dot_general(
                x[dev, q * HEADS:(q + 1) * HEADS, :], kc,
                (((1,), (1,)), ((), ())), preferred_element_type=F32))
        soft = []
        for s, (dev, q, length, base, c, at, rr) in zip(scores, todo):
            s = jnp.concatenate([
                s[a * held * gw:(a + 1) * held * gw, a * LANES:(a + 1) * LANES]
                for a in range(KV_HEADS // held)], axis=0)
            s = jnp.where(tok < length, s * (WIDTH ** -0.5), NEG)
            m = jnp.max(s, axis=-1, keepdims=True)
            w = jnp.where(tok < length, jnp.exp(s - m), 0.0).astype(BF)
            l = jnp.sum(w.astype(F32), axis=-1, keepdims=True)
            soft.append((m, w, l))
        for (m, w, l), (dev, q, length, base, c, at, rr) in zip(soft, todo):
            vb = kv[1, pl.ds(base, BLOCK_TOKENS), :]
            vc = jnp.concatenate([vb[:, k * WIDTH:(k + 1) * WIDTH] for k in range(KV_HEADS)], axis=0)
            wide = jnp.concatenate([
                jnp.concatenate([
                    w[a * held * gw:(a + 1) * held * gw] if b == a else blank
                    for b in range(KV_HEADS // held)], axis=1)
                for a in range(KV_HEADS // held)], axis=0)
            o = jnp.dot(wide, vc, preferred_element_type=F32)
            for grp in range(ngrp):
                ob[grp * g + step * CLASSES + c, at * hg:(at + 1) * hg, :] = o[grp * hg:(grp + 1) * hg].astype(BF)
        for grp in range(ngrp):
            send(step, grp).start()
        for c in range(CLASSES):
            top = jnp.zeros((HEADS, LANES), F32)
            tot = jnp.zeros((HEADS, LANES), F32)
            who = jnp.zeros((1, LANES), F32)
            for (m, w, l), (dev, q, length, base, cc, at, rr) in zip(soft, todo):
                if cc == c:
                    here = spot == at
                    top = jnp.where(here, m, top)
                    tot = jnp.where(here, l, tot)
                    who = jnp.where(here[0:1], rr.astype(F32), who)
            top = lump(top)
            tot = lump(tot)
            hi = top.astype(BF).astype(F32)
            mid = (top - hi).astype(BF).astype(F32)
            big = tot.astype(BF).astype(F32)
            for t, v in enumerate((hi, mid, top - hi - mid, big, tot - big, jnp.broadcast_to(who, top.shape))):
                sg[pl.ds((step * CLASSES + c) * STATS + t, ngrp, stride=g * STATS), :] = v
        return carry

    steps = g // CLASSES
    lax.fori_loop(0, steps, some, 0)
    ob[:, span:, :] = sg[...].reshape(n, STATS, LANES).astype(BF)
    last = pltpu.make_async_copy(ob.at[:, span:], out.at[:, span:], st)
    last.start()
    for step in range(steps):
        for grp in range(ngrp):
            send(step, grp).wait()
    last.wait()


def attend(n, slots, g, hg, block_len, asked, key_value_cache):
    pairs = n * slots
    span = hg * (pairs // g)
    sds = jax.ShapeDtypeStruct
    return call(
        functools.partial(attend_kernel, n, slots, g, hg),
        sds((n, span + STATS, LANES), BF), [HB, VM, VM],
        [
            pltpu.SMEM(block_len.shape, jnp.int32),
            pltpu.VMEM((slots * 8, LANES), jnp.int32),
            pltpu.SMEM((slots * 8, LANES), jnp.int32),
            pltpu.VMEM((n * STATS, LANES), F32),
            pltpu.VMEM((n, span + STATS, LANES), BF),
            pltpu.SemaphoreType.DMA((2,)),
            pltpu.SemaphoreType.DMA((g // CLASSES, n // g)),
            pltpu.SemaphoreType.DMA,
        ],
        out=ANY, flops=4 * HEADS * pairs * BLOCK_TOKENS * WIDTH, nbytes=COST,
    )(block_len, asked, key_value_cache)


def project_kernel(n, slots, g, hg, run, rows, x, *refs):
    pieces = refs[:g]
    outs = refs[g:g + n // g]
    sf, cm, ws, sp, ab, sem = refs[g + n // g:]
    fw = pieces[0].shape[0]
    me = lax.rem(lax.axis_index("section"), g)
    mine_group = lax.div(lax.axis_index("section"), g)
    loads = {}
    for i in list(range(2, g, 2)) + list(range(3, g, 2)) + [0, 1]:
        at = pl.multiple_of(lax.bitwise_xor(me, i) * fw, fw)
        loads[i] = pltpu.make_async_copy(pieces[i], ws.at[pl.ds(at, fw)], sem.at[i])
        loads[i].start()
    pairs = n * slots
    per = pairs // g
    span = hg * per
    cnt = n // g
    sf[...] = x[:, span:, :].astype(F32).reshape(n * STATS, LANES)
    m = (sf[pl.ds(0, n, stride=STATS), :] + sf[pl.ds(1, n, stride=STATS), :]
         + sf[pl.ds(2, n, stride=STATS), :])
    l = sf[pl.ds(3, n, stride=STATS), :] + sf[pl.ds(4, n, stride=STATS), :]
    rid = sf[pl.ds(5, n, stride=STATS), :]
    peak = jnp.zeros_like(m)
    for r in range(run):
        mine = rid == r
        top = jnp.max(jnp.where(mine, m, -3e38), axis=0, keepdims=True)
        peak = jnp.where(mine, top, peak)
    f = jnp.exp(m - peak)
    fl = f * l
    den = jnp.ones_like(m)
    for r in range(run):
        mine = rid == r
        tot = jnp.sum(jnp.where(mine, fl, 0.0), axis=0, keepdims=True)
        den = jnp.where(mine, tot, den)
    c = f / den
    lane = lax.broadcasted_iota(jnp.int32, (n, LANES), 1)
    inner = lax.rem(lane, span)
    hh = lax.rem(inner, hg)
    pl_ = lax.div(inner, hg)
    q = lax.div(pl_, cnt)
    s = lax.rem(pl_, cnt)
    local = rows * cnt
    target = hh * local + s * rows + q * run + rid.astype(jnp.int32)
    dpt = LANES // span
    total = hg * local
    row = lax.broadcasted_iota(jnp.int32, (total, LANES), 0)
    side = lax.div(lax.broadcasted_iota(jnp.int32, (1, LANES), 1), span)
    for t in range(n // dpt):
        blk_c = c[t * dpt:t * dpt + 1, :]
        blk_t = target[t * dpt:t * dpt + 1, :]
        for u in range(1, dpt):
            d = t * dpt + u
            blk_c = jnp.where(side == u, c[d:d + 1, :], blk_c)
            blk_t = jnp.where(side == u, target[d:d + 1, :], blk_t)
        cm[:, t * LANES:(t + 1) * LANES] = jnp.where(row == blk_t, blk_c, 0.0).astype(BF)
    a = x[:, 0:span, :].reshape(n * span, LANES)
    att = jnp.dot(cm[...], a, preferred_element_type=F32).astype(BF)
    ab[...] = jnp.concatenate([att[i * local:(i + 1) * local, :] for i in range(hg)], axis=1)
    for far in range(0, g, 2):
        loads[far].wait()
        loads[far + 1].wait()
        at = pl.multiple_of(lax.div(lax.bitwise_xor(me, far), 2) * (2 * fw), 2 * fw)
        for col in range(0, ws.shape[1], 512):
            p = jnp.dot(
                ab[:, pl.ds(at, 2 * fw)], ws[pl.ds(at, 2 * fw), col:col + 512],
                preferred_element_type=F32).reshape(cnt, rows, 512)
            if far:
                p = p + sp[:, :, col:col + 512]
            sp[:, :, col:col + 512] = p
    for j, out in enumerate(outs):
        out[...] = sp[lax.bitwise_xor(mine_group, j)].astype(BF)


def norm_kernel(count, index_in, *refs):
    x = refs[:count]
    res, gain, proj, out, nf, pb, ob, index, sem = refs[count:]
    get = pltpu.make_async_copy(index_in, index, sem.at[0])
    get.start()
    rows, width = res.shape
    acc = x[0][...].astype(F32)
    for i in range(1, count):
        acc = acc + x[i][...].astype(F32)
    p = acc.astype(BF)
    pb[...] = p
    put = pltpu.make_async_copy(pb, proj, sem.at[1])
    put.start()
    stream = res[...].astype(F32) + p.astype(F32)
    ms = jnp.mean(stream * stream, axis=-1, keepdims=True)
    nrm = stream * lax.rsqrt(ms + 1e-06) * gain[...]
    tiles = width // LANES
    for c in range(tiles):
        nf[pl.ds(c, rows, stride=tiles), :] = nrm[:, c * LANES:(c + 1) * LANES]
    if rows * index.shape[1] != out.shape[0]:
        ob[...] = jnp.zeros_like(ob)
    get.wait()
    for r in range(rows):
        tile = nf[r * tiles:(r + 1) * tiles, :].astype(BF)
        for k in range(index.shape[1]):
            ob[index[r, k]] = tile
    send = pltpu.make_async_copy(ob, out, sem.at[2])
    send.start()
    put.wait()
    send.wait()


def expert_kernel(x, wu, wg, wd, out, xf, xb, of, gb, db, sg, sd):
    m, tiles, _ = x.shape
    width, ffe = wu.shape
    gc = ffe // GATE_PARTS
    dc = width // DOWN_PARTS
    gate = [pltpu.make_async_copy(
        wg.at[:, pl.ds(i * gc, gc)], gb.at[:, pl.ds(i * gc, gc)], sg.at[i]) for i in range(GATE_PARTS)]
    down = [pltpu.make_async_copy(
        wd.at[:, pl.ds(i * dc, dc)], db.at[:, pl.ds(i * dc, dc)], sd.at[i]) for i in range(DOWN_PARTS)]
    for c in gate + down:
        c.start()
    xf[...] = x[...].astype(F32).reshape(m * tiles, LANES)
    for c in range(tiles):
        xb[:, c * LANES:(c + 1) * LANES] = xf[pl.ds(c, m, stride=tiles), :].astype(BF)
    ua = jnp.dot(xb[...], wu[...], preferred_element_type=F32)
    parts = []
    for i, c in enumerate(gate):
        c.wait()
        ga = jnp.dot(xb[...], gb[:, i * gc:(i + 1) * gc], preferred_element_type=F32)
        parts.append((ga / (1.0 + jnp.exp(-ga)) * ua[:, i * gc:(i + 1) * gc]).astype(BF))
    h = jnp.concatenate(parts, axis=1)
    for i, c in enumerate(down):
        c.wait()
        o = jnp.dot(h, db[:, i * dc:(i + 1) * dc], preferred_element_type=F32)
        for t in range(dc // LANES):
            of[pl.ds(i * dc // LANES + t, m, stride=tiles), :] = o[:, t * LANES:(t + 1) * LANES]
    out[...] = of[...].astype(BF).reshape(m, tiles, LANES)


def finish_kernel(index_in, rw_in, x, res, proj, out, acc, base, index, rw, sem):
    loads = [
        pltpu.make_async_copy(index_in, index, sem.at[0]),
        pltpu.make_async_copy(rw_in, rw, sem.at[1]),
    ]
    for c in loads:
        c.start()
    rows, width = res.shape
    tiles = width // LANES
    base[...] = res[...].astype(F32) + proj[...].astype(F32)
    for c in loads:
        c.wait()
    for r in range(rows):
        a = jnp.zeros((tiles, LANES), F32)
        for k in range(index.shape[1]):
            a = a + rw[r, k] * x[index[r, k]].astype(F32)
        acc[r * tiles:(r + 1) * tiles, :] = a
    for c in range(tiles):
        sl = slice(c * LANES, (c + 1) * LANES)
        out[:, sl] = (base[:, sl] + acc[pl.ds(c, rows, stride=tiles), :]).astype(BF)


def shards(
    queries,
    key_value_cache,
    block_ids,
    block_len,
    residual_in,
    out_weight,
    norm_gain,
    expert_ids,
    route_weight,
    w_gate,
    w_up,
    w_down,
):
    n = lax.axis_size("section")
    rows, _ = queries.shape
    picks = block_ids.shape[1]
    blocks = block_len.shape[0]
    width = residual_in.shape[1]
    run = n // picks
    slots = (rows + run - 1) // run
    g = GROUP
    fw = out_weight.shape[0]
    hg = g * fw // WIDTH
    pairs = n * slots
    per = pairs // g
    span = hg * per
    cnt = n // g
    tiles = width // LANES
    a2a = functools.partial(
        lax.all_to_all, axis_name="section", split_axis=0, concat_axis=0, tiled=True)
    sds = jax.ShapeDtypeStruct

    pieces = [None] * g
    for far in range(0, g, 2):
        if far:
            pieces[far] = lax.ppermute(out_weight, "section", [(i, i ^ far) for i in range(n)])
        else:
            pieces[0] = out_weight
    for far in range(0, g, 2):
        pieces[far + 1] = lax.ppermute(pieces[far], "section", [(i, i ^ 1) for i in range(n)])
    (cache,) = stage(key_value_cache)
    flat = expert_ids.reshape(-1)
    place = jnp.arange(flat.shape[0])
    slot = jnp.sum(
        (flat[:, None] == flat[None, :]) & (place[:, None] > place[None, :]), axis=1
    ).astype(jnp.int32)
    index = (flat * CAP + slot).reshape(expert_ids.shape)

    chunk = slots * HEADS + 8
    sent = call(
        functools.partial(pack_kernel, run, slots, blocks),
        sds((n, chunk, LANES), BF), [HB, HB],
        [
            pltpu.SMEM(block_ids.shape, jnp.int32),
            pltpu.VMEM(queries.shape, BF),
            pltpu.VMEM((rows * HEADS, LANES), F32),
            pltpu.VMEM((n, 8, LANES), F32),
            pltpu.VMEM((n, chunk, LANES), BF),
            pltpu.SemaphoreType.DMA((2,)),
            pltpu.SemaphoreType.DMA((slots,)),
        ],
        nbytes=COST, room=60, out=ANY,
    )(block_ids, queries)
    asked = a2a(sent)
    parts = attend(n, slots, g, hg, block_len, asked, cache)
    back = a2a(parts)
    local = rows * cnt
    partial = call(
        functools.partial(project_kernel, n, slots, g, hg, run, rows),
        (sds((rows, width), BF),) * cnt, [VM] + [ANY] * g,
        [
            pltpu.VMEM((n * STATS, LANES), F32),
            pltpu.VMEM((hg * local, n * span), BF),
            pltpu.VMEM((g * fw, width), BF),
            pltpu.VMEM((cnt, rows, width), F32),
            pltpu.VMEM((local, g * fw), BF),
            pltpu.SemaphoreType.DMA((g,)),
        ],
        flops=2 * local * g * fw * width, nbytes=COST, room=PROJECT_ROOM,
    )(back, *pieces)
    (up_w,) = stage(w_up, after=(partial[0],))
    summed = [partial[0]]
    for j in range(cnt - 1, 0, -1):
        summed.append(lax.ppermute(partial[j], "section", [(i, i ^ (j * g)) for i in range(n)]))
    experts = n * w_gate.shape[0]
    attn_proj, routed = call(
        functools.partial(norm_kernel, cnt),
        (sds((rows, width), BF), sds((experts * CAP, tiles, LANES), BF)), [ANY] + [VM] * (cnt + 2),
        [
            pltpu.VMEM((rows * tiles, LANES), F32),
            pltpu.VMEM((rows, width), BF),
            pltpu.VMEM((experts * CAP, tiles, LANES), BF),
            pltpu.SMEM(index.shape, jnp.int32),
            pltpu.SemaphoreType.DMA((3,)),
        ],
        out=(ANY, ANY), nbytes=COST,
    )(index, *summed, residual_in, norm_gain.reshape(1, width))
    arrived = a2a(routed)
    ffe = w_gate.shape[2]
    slots_in = n * CAP

    def run_expert(xin, wu, wg, wd):
        return call(
            expert_kernel,
            sds((slots_in, tiles, LANES), BF), [VM, VM, ANY, ANY],
            [
                pltpu.VMEM((slots_in * tiles, LANES), F32),
                pltpu.VMEM((slots_in, width), BF),
                pltpu.VMEM((slots_in * tiles, LANES), F32),
                pltpu.VMEM((width, ffe), BF),
                pltpu.VMEM((ffe, width), BF),
                pltpu.SemaphoreType.DMA((GATE_PARTS,)),
                pltpu.SemaphoreType.DMA((DOWN_PARTS,)),
            ],
            room=49, flops=6 * slots_in * width * ffe, nbytes=6 * width * ffe,
        )(xin, wu, wg, wd)

    per_device = w_gate.shape[0]
    if per_device == 1:
        done = run_expert(arrived, up_w[0], w_gate[0], w_down[0])
    else:
        split = arrived.reshape(n, per_device, CAP, tiles, LANES)
        done = jnp.stack([
            run_expert(split[:, e].reshape(slots_in, tiles, LANES), up_w[e], w_gate[e], w_down[e])
            .reshape(n, CAP, tiles, LANES) for e in range(per_device)], axis=1).reshape(arrived.shape)
    returned = a2a(done)
    layer_out = call(
        finish_kernel,
        sds((rows, width), BF), [ANY, ANY, VM, VM, VM],
        [
            pltpu.VMEM((rows * tiles, LANES), F32),
            pltpu.VMEM((rows, width), F32),
            pltpu.SMEM(index.shape, jnp.int32),
            pltpu.SMEM(route_weight.shape, F32),
            pltpu.SemaphoreType.DMA((2,)),
        ],
        nbytes=1 << 19,
    )(index, route_weight, returned, residual_in, attn_proj)
    return (attn_proj, layer_out)


def solution(mesh):
    both = P(("groups", "section"), None)
    placed = (
        both,
        P(None, ("groups", "section"), None),
        both,
        P(("groups", "section")),
        both,
        P("section", None),
        P(),
        both,
        both,
        P("section", None, None),
        P("section", None, None),
        P("section", None, None),
    )

    return jax.shard_map(
        shards,
        mesh=mesh,
        in_specs=placed,
        out_specs=(both, both),
        check_vma=False,
    )
```

```python
import functools

import jax
import jax.numpy as jnp
from jax import lax
from jax.experimental import pallas as pl
from jax.experimental.pallas import tpu as pltpu
from jax.sharding import PartitionSpec as P


HEADS = 32
KV_HEADS = 4
WIDTH = 128
CAP = 2
BLOCK_TOKENS = 64
LANES = 128
GROUP = 8
STATS = 8
TILE = 2
PART = 4
CLASSES = 4
NEG = -1e30
COST = 1 << 26
PROJECT_ROOM = 16
GATE_PARTS = 3
DOWN_PARTS = 4
BF = jnp.bfloat16
F32 = jnp.float32

VM = pl.BlockSpec(memory_space=pltpu.VMEM)
SM = pl.BlockSpec(memory_space=pltpu.SMEM)
HB = pl.BlockSpec(memory_space=pltpu.HBM)
ANY = pl.BlockSpec(memory_space=pl.ANY)


def call(kernel, out_shape, in_specs, scratch, flops=0, nbytes=0, room=8, out=None):
    return pl.pallas_call(
        kernel,
        out_shape=out_shape,
        in_specs=in_specs,
        out_specs=out if out is not None else jax.tree.map(lambda _: VM, out_shape),
        scratch_shapes=scratch,
        compiler_params=pltpu.CompilerParams(vmem_limit_bytes=room << 20),
        cost_estimate=pl.CostEstimate(flops=flops, bytes_accessed=nbytes, transcendentals=0),
    )


def stage_kernel(count, *refs):
    sem = refs[-1]
    outs = refs[-1 - count:-1]
    copies = [pltpu.make_async_copy(refs[i], outs[i], sem.at[i]) for i in range(count)]
    for c in copies:
        c.start()
    for c in copies:
        c.wait()


def stage(*arrays, after=()):
    count = len(arrays)
    nbytes = sum(a.size * a.dtype.itemsize for a in arrays)
    return call(
        functools.partial(stage_kernel, count),
        tuple(jax.ShapeDtypeStruct(a.shape, a.dtype) for a in arrays),
        [ANY] * (count + len(after)), [pltpu.SemaphoreType.DMA((count,))],
        nbytes=nbytes,
    )(*arrays, *after)


def pack_kernel(run, slots, blocks, ids_in, q_in, out, ids, q, qs, meta, ob, sem, so):
    rows = q.shape[0]
    picks = ids.shape[1]
    get_ids = pltpu.make_async_copy(ids_in, ids, sem.at[0])
    get_q = pltpu.make_async_copy(q_in, q, sem.at[1])
    get_ids.start()
    get_q.start()
    meta[...] = jnp.zeros_like(meta)
    if rows * picks != out.shape[0] * slots:
        ob[...] = jnp.zeros_like(ob)
    get_q.wait()
    for h in range(HEADS):
        qs[pl.ds(h, rows, stride=HEADS), :] = q[:, h * WIDTH:(h + 1) * WIDTH].astype(F32)
    get_ids.wait()
    lane = lax.broadcasted_iota(jnp.int32, (1, LANES), 1)
    sends = []
    for r in range(rows):
        tile = qs[r * HEADS:(r + 1) * HEADS, :].astype(BF).reshape(HEADS // TILE, TILE, LANES)
        slot = r // run
        for j in range(picks):
            b = ids[r, j]
            dev = lax.div(b, blocks)
            local = b - dev * blocks
            ob[dev, slot * HEADS // TILE:(slot + 1) * HEADS // TILE] = tile
            meta[dev, slot:slot + 1, :] = jnp.where(
                lane == 0, local + 1, jnp.where(lane == 1, r % run, 0)
            ).astype(F32)
        if r % run == run - 1 or r == rows - 1:
            if r == rows - 1:
                ob[:, slots * HEADS // TILE] = meta[:, 0:TILE].astype(BF)
                part = slice(slot * HEADS // TILE, slots * HEADS // TILE + 1)
            else:
                part = slice(slot * HEADS // TILE, (slot + 1) * HEADS // TILE)
            sends.append(pltpu.make_async_copy(ob.at[:, part], out.at[:, part], so.at[slot]))
            sends[-1].start()
    for c in sends:
        c.wait()


def attend_kernel(n, slots, g, hg, lens_in, x, kv, out, lens, mv, ms, sg, ob, sem, so, st):
    get_lens = pltpu.make_async_copy(lens_in, lens, sem.at[1])
    get_lens.start()
    cnt = n // g
    ngrp = n // g
    per = slots * cnt
    qrows = slots * HEADS
    gw = HEADS // KV_HEADS
    span = hg * per

    for q in range(slots):
        for d in range(n):
            sg[d:d + 1, :] = x[d, qrows // TILE, q:q + 1, :].astype(F32)
        mv[q * 8:(q + 1) * 8, 0:n] = jnp.transpose(sg[0:n, :])[0:8, :].astype(jnp.int32)
    table = pltpu.make_async_copy(mv, ms, sem.at[0])
    table.start()
    sg[...] = jnp.zeros_like(sg)
    lane = lax.broadcasted_iota(jnp.int32, (HEADS, LANES), 1)
    spot = lax.rem(lax.div(lane, hg), per)
    own = lax.rem(lane, hg) == lax.rem(lax.broadcasted_iota(jnp.int32, lane.shape, 0), hg)
    held = LANES // BLOCK_TOKENS
    owner = lax.rem(lax.div(lax.broadcasted_iota(jnp.int32, lane.shape, 0), gw), held)
    tok = jnp.where(lax.div(lane, BLOCK_TOKENS) == owner, lax.rem(lane, BLOCK_TOKENS), BLOCK_TOKENS)
    blank = jnp.zeros((held * gw, LANES), BF)
    table.wait()
    get_lens.wait()

    def send(step, grp):
        first = grp * g + step * CLASSES
        return pltpu.make_async_copy(
            ob.at[pl.ds(first, CLASSES), 0:span // PART],
            out.at[pl.ds(first, CLASSES), 0:span // PART], so.at[step, grp])

    def lump(v):
        v = jnp.where(own, v, 0.0)
        return jnp.concatenate(
            [jnp.sum(v[a:a + hg], axis=0, keepdims=True) for a in range(0, HEADS, hg)], axis=0)

    def some(step, carry):
        todo = []
        for c in range(CLASSES):
            i = step * CLASSES + c
            for q in range(slots):
                for s in range(cnt):
                    dev = s * g + i
                    blk = ms[q * 8, dev] - 1
                    safe = jnp.maximum(blk, 0)
                    length = jnp.where(blk >= 0, lens[safe], 0)
                    base = pl.multiple_of(safe * BLOCK_TOKENS, BLOCK_TOKENS)
                    todo.append((dev, q, length, base, c, q * cnt + s, ms[q * 8 + 1, dev]))
        scores = []
        for dev, q, length, base, c, at, rr in todo:
            kb = kv[0, pl.ds(base, BLOCK_TOKENS), :]
            kc = jnp.concatenate([kb[:, k * WIDTH:(k + 1) * WIDTH] for k in range(KV_HEADS)], axis=0)
            scores.append(lax.dot_general(
                x[dev, q * HEADS // TILE:(q + 1) * HEADS // TILE].reshape(HEADS, WIDTH), kc,
                (((1,), (1,)), ((), ())), preferred_element_type=F32))
        soft = []
        for s, (dev, q, length, base, c, at, rr) in zip(scores, todo):
            s = jnp.concatenate([
                s[a * held * gw:(a + 1) * held * gw, a * LANES:(a + 1) * LANES]
                for a in range(KV_HEADS // held)], axis=0)
            s = jnp.where(tok < length, s * (WIDTH ** -0.5), NEG)
            m = jnp.max(s, axis=-1, keepdims=True)
            w = jnp.where(tok < length, jnp.exp(s - m), 0.0).astype(BF)
            l = jnp.sum(w.astype(F32), axis=-1, keepdims=True)
            soft.append((m, w, l))
        for (m, w, l), (dev, q, length, base, c, at, rr) in zip(soft, todo):
            vb = kv[1, pl.ds(base, BLOCK_TOKENS), :]
            vc = jnp.concatenate([vb[:, k * WIDTH:(k + 1) * WIDTH] for k in range(KV_HEADS)], axis=0)
            wide = jnp.concatenate([
                jnp.concatenate([
                    w[a * held * gw:(a + 1) * held * gw] if b == a else blank
                    for b in range(KV_HEADS // held)], axis=1)
                for a in range(KV_HEADS // held)], axis=0)
            o = jnp.dot(wide, vc, preferred_element_type=F32)
            for grp in range(ngrp):
                ob[grp * g + step * CLASSES + c, at * hg // PART:(at + 1) * hg // PART] = (
                    o[grp * hg:(grp + 1) * hg].astype(BF).reshape(hg // PART, PART, LANES))
        for grp in range(ngrp):
            send(step, grp).start()
        for c in range(CLASSES):
            top = jnp.zeros((HEADS, LANES), F32)
            tot = jnp.zeros((HEADS, LANES), F32)
            who = jnp.zeros((1, LANES), F32)
            for (m, w, l), (dev, q, length, base, cc, at, rr) in zip(soft, todo):
                if cc == c:
                    here = spot == at
                    top = jnp.where(here, m, top)
                    tot = jnp.where(here, l, tot)
                    who = jnp.where(here[0:1], rr.astype(F32), who)
            top = lump(top)
            tot = lump(tot)
            hi = top.astype(BF).astype(F32)
            mid = (top - hi).astype(BF).astype(F32)
            big = tot.astype(BF).astype(F32)
            lower = lane[0:ngrp] < LANES // 2
            pairs_of = ((hi, big), (mid, tot - big), (top - hi - mid, jnp.broadcast_to(who, top.shape)))
            for t, (u, v) in enumerate(pairs_of):
                sg[pl.ds((step * CLASSES + c) * PART + t, ngrp, stride=g * PART), :] = jnp.where(lower, u, v)
        return carry

    steps = g // CLASSES
    lax.fori_loop(0, steps, some, 0)
    ob[:, span // PART] = sg[0:n * PART, :].reshape(n, PART, LANES).astype(BF)
    last = pltpu.make_async_copy(ob.at[:, span // PART], out.at[:, span // PART], st)
    last.start()
    for step in range(steps):
        for grp in range(ngrp):
            send(step, grp).wait()
    last.wait()


def attend(n, slots, g, hg, block_len, asked, key_value_cache):
    pairs = n * slots
    span = hg * (pairs // g)
    sds = jax.ShapeDtypeStruct
    return call(
        functools.partial(attend_kernel, n, slots, g, hg),
        sds((n, span // PART + 1, PART, LANES), BF), [HB, VM, VM],
        [
            pltpu.SMEM(block_len.shape, jnp.int32),
            pltpu.VMEM((slots * 8, LANES), jnp.int32),
            pltpu.SMEM((slots * 8, LANES), jnp.int32),
            pltpu.VMEM((n * STATS, LANES), F32),
            pltpu.VMEM((n, span // PART + 1, PART, LANES), BF),
            pltpu.SemaphoreType.DMA((2,)),
            pltpu.SemaphoreType.DMA((g // CLASSES, n // g)),
            pltpu.SemaphoreType.DMA,
        ],
        out=ANY, flops=4 * HEADS * pairs * BLOCK_TOKENS * WIDTH, nbytes=COST,
    )(block_len, asked, key_value_cache)


def project_kernel(n, slots, g, hg, run, rows, x, *refs):
    pieces = refs[:g]
    outs = refs[g:g + n // g]
    sf, cm, ws, sp, ab, sem = refs[g + n // g:]
    fw = pieces[0].shape[0]
    me = lax.rem(lax.axis_index("section"), g)
    mine_group = lax.div(lax.axis_index("section"), g)
    loads = {}
    for i in list(range(2, g, 2)) + list(range(3, g, 2)) + [0, 1]:
        at = pl.multiple_of(lax.bitwise_xor(me, i) * fw, fw)
        loads[i] = pltpu.make_async_copy(pieces[i], ws.at[pl.ds(at, fw)], sem.at[i])
        loads[i].start()
    pairs = n * slots
    per = pairs // g
    span = hg * per
    cnt = n // g
    sf[...] = x[:, span // PART].astype(F32).reshape(n * PART, LANES)
    first, second, third = (sf[pl.ds(t, n, stride=PART), :] for t in range(3))
    lower = lax.broadcasted_iota(jnp.int32, (n, LANES), 1) < LANES // 2

    def turn(v):
        return pltpu.roll(v, LANES // 2, 1)

    m = first + second + third
    m = jnp.where(lower, m, turn(m))
    l = first + second
    l = jnp.where(lower, turn(l), l)
    rid = jnp.where(lower, turn(third), third)
    peak = jnp.zeros_like(m)
    for r in range(run):
        mine = rid == r
        top = jnp.max(jnp.where(mine, m, -3e38), axis=0, keepdims=True)
        peak = jnp.where(mine, top, peak)
    f = jnp.exp(m - peak)
    fl = f * l
    den = jnp.ones_like(m)
    for r in range(run):
        mine = rid == r
        tot = jnp.sum(jnp.where(mine, fl, 0.0), axis=0, keepdims=True)
        den = jnp.where(mine, tot, den)
    c = f / den
    lane = lax.broadcasted_iota(jnp.int32, (n, LANES), 1)
    inner = lax.rem(lane, span)
    hh = lax.rem(inner, hg)
    pl_ = lax.div(inner, hg)
    q = lax.div(pl_, cnt)
    s = lax.rem(pl_, cnt)
    local = rows * cnt
    target = hh * local + s * rows + q * run + rid.astype(jnp.int32)
    dpt = LANES // span
    total = hg * local
    row = lax.broadcasted_iota(jnp.int32, (total, LANES), 0)
    side = lax.div(lax.broadcasted_iota(jnp.int32, (1, LANES), 1), span)
    for t in range(n // dpt):
        blk_c = c[t * dpt:t * dpt + 1, :]
        blk_t = target[t * dpt:t * dpt + 1, :]
        for u in range(1, dpt):
            d = t * dpt + u
            blk_c = jnp.where(side == u, c[d:d + 1, :], blk_c)
            blk_t = jnp.where(side == u, target[d:d + 1, :], blk_t)
        cm[:, t * LANES:(t + 1) * LANES] = jnp.where(row == blk_t, blk_c, 0.0).astype(BF)
    a = x[:, 0:span // PART].reshape(n * span, LANES)
    att = jnp.dot(cm[...], a, preferred_element_type=F32).astype(BF)
    ab[...] = jnp.concatenate([att[i * local:(i + 1) * local, :] for i in range(hg)], axis=1)
    for far in range(0, g, 2):
        loads[far].wait()
        loads[far + 1].wait()
        at = pl.multiple_of(lax.div(lax.bitwise_xor(me, far), 2) * (2 * fw), 2 * fw)
        for col in range(0, ws.shape[1], 512):
            p = jnp.dot(
                ab[:, pl.ds(at, 2 * fw)], ws[pl.ds(at, 2 * fw), col:col + 512],
                preferred_element_type=F32).reshape(cnt, rows, 512)
            if far:
                p = p + sp[:, :, col:col + 512]
            sp[:, :, col:col + 512] = p
    for j, out in enumerate(outs):
        out[...] = sp[lax.bitwise_xor(mine_group, j)].astype(BF)


def norm_kernel(count, index_in, *refs):
    x = refs[:count]
    res, gain, proj, out, nf, pb, ob, index, sem = refs[count:]
    get = pltpu.make_async_copy(index_in, index, sem.at[0])
    get.start()
    rows, width = res.shape
    acc = x[0][...].astype(F32)
    for i in range(1, count):
        acc = acc + x[i][...].astype(F32)
    p = acc.astype(BF)
    pb[...] = p
    put = pltpu.make_async_copy(pb, proj, sem.at[1])
    put.start()
    stream = res[...].astype(F32) + p.astype(F32)
    ms = jnp.mean(stream * stream, axis=-1, keepdims=True)
    nrm = stream * lax.rsqrt(ms + 1e-06) * gain[...]
    tiles = width // LANES
    for c in range(tiles):
        nf[pl.ds(c, rows, stride=tiles), :] = nrm[:, c * LANES:(c + 1) * LANES]
    if rows * index.shape[1] != out.shape[0]:
        ob[...] = jnp.zeros_like(ob)
    get.wait()
    for r in range(rows):
        tile = nf[r * tiles:(r + 1) * tiles, :].astype(BF)
        for k in range(index.shape[1]):
            ob[index[r, k]] = tile
    send = pltpu.make_async_copy(ob, out, sem.at[2])
    send.start()
    put.wait()
    send.wait()


def expert_kernel(x, wu, wg, wd, out, xf, xb, of, gb, db, sg, sd):
    m, tiles, _ = x.shape
    width, ffe = wu.shape
    gc = ffe // GATE_PARTS
    dc = width // DOWN_PARTS
    gate = [pltpu.make_async_copy(
        wg.at[:, pl.ds(i * gc, gc)], gb.at[:, pl.ds(i * gc, gc)], sg.at[i]) for i in range(GATE_PARTS)]
    down = [pltpu.make_async_copy(
        wd.at[:, pl.ds(i * dc, dc)], db.at[:, pl.ds(i * dc, dc)], sd.at[i]) for i in range(DOWN_PARTS)]
    for c in gate + down:
        c.start()
    xf[...] = x[...].astype(F32).reshape(m * tiles, LANES)
    for c in range(tiles):
        xb[:, c * LANES:(c + 1) * LANES] = xf[pl.ds(c, m, stride=tiles), :].astype(BF)
    ua = jnp.dot(xb[...], wu[...], preferred_element_type=F32)
    parts = []
    for i, c in enumerate(gate):
        c.wait()
        ga = jnp.dot(xb[...], gb[:, i * gc:(i + 1) * gc], preferred_element_type=F32)
        parts.append((ga / (1.0 + jnp.exp(-ga)) * ua[:, i * gc:(i + 1) * gc]).astype(BF))
    h = jnp.concatenate(parts, axis=1)
    for i, c in enumerate(down):
        c.wait()
        o = jnp.dot(h, db[:, i * dc:(i + 1) * dc], preferred_element_type=F32)
        for t in range(dc // LANES):
            of[pl.ds(i * dc // LANES + t, m, stride=tiles), :] = o[:, t * LANES:(t + 1) * LANES]
    out[...] = of[...].astype(BF).reshape(m, tiles, LANES)


def finish_kernel(index_in, rw_in, x, res, proj, out, acc, base, index, rw, sem):
    loads = [
        pltpu.make_async_copy(index_in, index, sem.at[0]),
        pltpu.make_async_copy(rw_in, rw, sem.at[1]),
    ]
    for c in loads:
        c.start()
    rows, width = res.shape
    tiles = width // LANES
    base[...] = res[...].astype(F32) + proj[...].astype(F32)
    for c in loads:
        c.wait()
    for r in range(rows):
        a = jnp.zeros((tiles, LANES), F32)
        for k in range(index.shape[1]):
            a = a + rw[r, k] * x[index[r, k]].astype(F32)
        acc[r * tiles:(r + 1) * tiles, :] = a
    for c in range(tiles):
        sl = slice(c * LANES, (c + 1) * LANES)
        out[:, sl] = (base[:, sl] + acc[pl.ds(c, rows, stride=tiles), :]).astype(BF)


def shards(
    queries,
    key_value_cache,
    block_ids,
    block_len,
    residual_in,
    out_weight,
    norm_gain,
    expert_ids,
    route_weight,
    w_gate,
    w_up,
    w_down,
):
    n = lax.axis_size("section")
    rows, _ = queries.shape
    picks = block_ids.shape[1]
    blocks = block_len.shape[0]
    width = residual_in.shape[1]
    run = n // picks
    slots = (rows + run - 1) // run
    g = GROUP
    fw = out_weight.shape[0]
    hg = g * fw // WIDTH
    pairs = n * slots
    per = pairs // g
    span = hg * per
    cnt = n // g
    tiles = width // LANES
    a2a = functools.partial(
        lax.all_to_all, axis_name="section", split_axis=0, concat_axis=0, tiled=True)
    sds = jax.ShapeDtypeStruct

    pieces = [None] * g
    for far in range(0, g, 2):
        if far:
            pieces[far] = lax.ppermute(out_weight, "section", [(i, i ^ far) for i in range(n)])
        else:
            pieces[0] = out_weight
    for far in range(0, g, 2):
        pieces[far + 1] = lax.ppermute(pieces[far], "section", [(i, i ^ 1) for i in range(n)])
    (cache,) = stage(key_value_cache)
    flat = expert_ids.reshape(-1)
    place = jnp.arange(flat.shape[0])
    slot = jnp.sum(
        (flat[:, None] == flat[None, :]) & (place[:, None] > place[None, :]), axis=1
    ).astype(jnp.int32)
    index = (flat * CAP + slot).reshape(expert_ids.shape)

    chunk = slots * HEADS // TILE + 1
    sent = call(
        functools.partial(pack_kernel, run, slots, blocks),
        sds((n, chunk, TILE, LANES), BF), [HB, HB],
        [
            pltpu.SMEM(block_ids.shape, jnp.int32),
            pltpu.VMEM(queries.shape, BF),
            pltpu.VMEM((rows * HEADS, LANES), F32),
            pltpu.VMEM((n, 8, LANES), F32),
            pltpu.VMEM((n, chunk, TILE, LANES), BF),
            pltpu.SemaphoreType.DMA((2,)),
            pltpu.SemaphoreType.DMA((slots,)),
        ],
        nbytes=COST, room=60, out=ANY,
    )(block_ids, queries)
    asked = a2a(sent)
    parts = attend(n, slots, g, hg, block_len, asked, cache)
    back = a2a(parts)
    local = rows * cnt
    partial = call(
        functools.partial(project_kernel, n, slots, g, hg, run, rows),
        (sds((rows, width), BF),) * cnt, [VM] + [ANY] * g,
        [
            pltpu.VMEM((n * PART, LANES), F32),
            pltpu.VMEM((hg * local, n * span), BF),
            pltpu.VMEM((g * fw, width), BF),
            pltpu.VMEM((cnt, rows, width), F32),
            pltpu.VMEM((local, g * fw), BF),
            pltpu.SemaphoreType.DMA((g,)),
        ],
        flops=2 * local * g * fw * width, nbytes=COST, room=PROJECT_ROOM,
    )(back, *pieces)
    (up_w,) = stage(w_up, after=(partial[0],))
    summed = [partial[0]]
    for j in range(cnt - 1, 0, -1):
        summed.append(lax.ppermute(partial[j], "section", [(i, i ^ (j * g)) for i in range(n)]))
    experts = n * w_gate.shape[0]
    attn_proj, routed = call(
        functools.partial(norm_kernel, cnt),
        (sds((rows, width), BF), sds((experts * CAP, tiles, LANES), BF)), [ANY] + [VM] * (cnt + 2),
        [
            pltpu.VMEM((rows * tiles, LANES), F32),
            pltpu.VMEM((rows, width), BF),
            pltpu.VMEM((experts * CAP, tiles, LANES), BF),
            pltpu.SMEM(index.shape, jnp.int32),
            pltpu.SemaphoreType.DMA((3,)),
        ],
        out=(ANY, ANY), nbytes=COST,
    )(index, *summed, residual_in, norm_gain.reshape(1, width))
    arrived = a2a(routed)
    ffe = w_gate.shape[2]
    slots_in = n * CAP

    def run_expert(xin, wu, wg, wd):
        return call(
            expert_kernel,
            sds((slots_in, tiles, LANES), BF), [VM, VM, ANY, ANY],
            [
                pltpu.VMEM((slots_in * tiles, LANES), F32),
                pltpu.VMEM((slots_in, width), BF),
                pltpu.VMEM((slots_in * tiles, LANES), F32),
                pltpu.VMEM((width, ffe), BF),
                pltpu.VMEM((ffe, width), BF),
                pltpu.SemaphoreType.DMA((GATE_PARTS,)),
                pltpu.SemaphoreType.DMA((DOWN_PARTS,)),
            ],
            room=49, flops=6 * slots_in * width * ffe, nbytes=6 * width * ffe,
        )(xin, wu, wg, wd)

    per_device = w_gate.shape[0]
    if per_device == 1:
        done = run_expert(arrived, up_w[0], w_gate[0], w_down[0])
    else:
        split = arrived.reshape(n, per_device, CAP, tiles, LANES)
        done = jnp.stack([
            run_expert(split[:, e].reshape(slots_in, tiles, LANES), up_w[e], w_gate[e], w_down[e])
            .reshape(n, CAP, tiles, LANES) for e in range(per_device)], axis=1).reshape(arrived.shape)
    returned = a2a(done)
    layer_out = call(
        finish_kernel,
        sds((rows, width), BF), [ANY, ANY, VM, VM, VM],
        [
            pltpu.VMEM((rows * tiles, LANES), F32),
            pltpu.VMEM((rows, width), F32),
            pltpu.SMEM(index.shape, jnp.int32),
            pltpu.SMEM(route_weight.shape, F32),
            pltpu.SemaphoreType.DMA((2,)),
        ],
        nbytes=1 << 19,
    )(index, route_weight, returned, residual_in, attn_proj)
    return (attn_proj, layer_out)


def solution(mesh):
    both = P(("groups", "section"), None)
    placed = (
        both,
        P(None, ("groups", "section"), None),
        both,
        P(("groups", "section")),
        both,
        P("section", None),
        P(),
        both,
        both,
        P("section", None, None),
        P("section", None, None),
        P("section", None, None),
    )

    return jax.shard_map(
        shards,
        mesh=mesh,
        in_specs=placed,
        out_specs=(both, both),
        check_vma=False,
    )
```
